32 devices in a mesh: tile: 8 (over y, x, core), depth: 4 (over z).
Axes of the slice: x: 2, y: 2, z: 4, core: 2. Of those that a mesh axis runs over, the one named last changes fastest.
Arguments:
- features: bfloat16 [4, 2048, 128], P('depth', 'tile'), may hold values from -4 to 4
- logits: float32 [4, 2048], P('depth', 'tile'), may hold values from -2.75 to 5.5
- geometry: float32 [2, 4, 5, 2048], P(None, 'depth', None, 'tile'), may hold values from -0.6 to 32, as said below
- dest_slot: int32 [2, 4, 2048], P(None, 'depth', 'tile'), may hold values from -1 to 2047, as said below
- target: bfloat16 [2, 16, 128, 1024], P(None, 'tile'), may hold values from -3 to 3
Outputs:
- images: bfloat16 [2, 16, 128, 1024], P(None, 'tile', None, 'depth')
- new_features: bfloat16 [4, 2048, 128], P('depth', 'tile')
- new_logits: float32 [4, 2048], P('depth', 'tile')
- shape_grads: float32 [2, 4, 5, 2048], P(None, 'depth', None, 'tile')
The draws below stay inside these ranges and needn't reach their ends.
Inputs may be any that keep to these rules, and one draw needn't show every extreme that they name: `dest_slot`: for each view and layer no two splats share a slot; -1 marks a splat outside the view; a splat's place within its tile is its front-to-back order. At most 32 splats of one layer held by one index of tile go to the tiles of one index of tile, and in every view and layer there is an index of tile whose tiles receive exactly 32 from every owner, so that all their slots are used. `geometry`: components 0 and 1 are a splat's centre in pixels within its tile, from 0 to 32; components 2 and 3 lie in -0.5 to 2.0; component 4 in -0.6 to 0.6.
All inputs are finite; a program needn't handle non-finite values.
Results may differ from the reference program's by a relative error of at most 0.0073.
Values may be sent and summed in bfloat16 or wider, within the bound.
A program may use at most 64 MiB of HBM per device.

```python
import jax
import jax.numpy as jnp
from jax import lax

F = 128
W = 32
S = 128
VIEWS = 2
P_SIZE = 1024
LAYERS = 4
TILES = 16
OWN = 256
SPLATS = 2048
CAP = 32
N_TILE = 8


def draw_logits(key, part):
    key_base, key_flag, key_high = jax.random.split(jax.random.fold_in(key, 11), 3)
    base_draw = jax.random.uniform(key_base, (LAYERS, SPLATS), jnp.float32)
    flag_draw = jax.random.uniform(key_flag, (LAYERS, SPLATS), jnp.float32)
    high_draw = jax.random.uniform(key_high, (LAYERS, SPLATS), jnp.float32)
    high = 5.0 + 0.5 * high_draw
    low = -2.75 + 1.6 * base_draw
    opaque = flag_draw < 1.0 / 32.0
    return jnp.where(opaque, high, low)


def draw_geometry(key, part):
    key_mean, key_scale, key_corr = jax.random.split(jax.random.fold_in(key, 23), 3)
    means = jax.random.uniform(key_mean, (VIEWS, LAYERS, 2, SPLATS), jnp.float32) * W
    scale_draw = jax.random.uniform(key_scale, (VIEWS, LAYERS, 2, SPLATS), jnp.float32)
    corr_draw = jax.random.uniform(key_corr, (VIEWS, LAYERS, 1, SPLATS), jnp.float32)
    scales = -0.5 + 2.5 * scale_draw
    corr = 0.6 * (2.0 * corr_draw - 1.0)
    return jnp.concatenate([means, scales, corr], axis=2)


def one_layer_slots(layer_key):
    key_counts, key_hot, key_owner, key_recv = jax.random.split(layer_key, 4)
    counts = jax.random.randint(key_counts, (N_TILE, N_TILE), 1, CAP + 1)
    hottest = jax.random.randint(key_hot, (), 0, N_TILE)
    counts = jnp.where(jnp.arange(N_TILE)[None, :] == hottest, CAP, counts).astype(jnp.int32)
    ends = jnp.cumsum(counts, axis=1)
    starts = ends - counts
    arrivals = jnp.cumsum(counts, axis=0) - counts
    recv_table = jax.vmap(lambda table_key: jax.random.permutation(table_key, OWN))(jax.random.split(key_recv, N_TILE))
    positions = jnp.arange(OWN, dtype=jnp.int32)

    def owner_row(owner, owner_key):
        receiver = jnp.sum((positions[:, None] >= ends[owner][None, :]).astype(jnp.int32), axis=1)
        visible = receiver < N_TILE
        safe = jnp.minimum(receiver, N_TILE - 1)
        place_in = positions - starts[owner][safe]
        arrival = jnp.clip(arrivals[owner][safe] + place_in, 0, OWN - 1)
        local_slot = recv_table[safe, arrival]
        value = jnp.where(visible, safe * OWN + local_slot, -1).astype(jnp.int32)
        shuffle = jax.random.permutation(owner_key, OWN)
        return jnp.zeros((OWN,), jnp.int32).at[shuffle].set(value)
    rows = jax.vmap(owner_row)(jnp.arange(N_TILE, dtype=jnp.int32), jax.random.split(key_owner, N_TILE))
    return rows.reshape(SPLATS)


def draw_dest_slot(key, part):
    layer_keys = jax.random.split(jax.random.fold_in(key, 37), VIEWS * LAYERS)
    slots = jax.vmap(one_layer_slots)(layer_keys)
    return slots.reshape(VIEWS, LAYERS, SPLATS)


def shard_levels(rng, dims, cuts, low, largest):
    def one(position, blocks):
        heights = jax.random.uniform(jax.random.fold_in(jax.random.fold_in(rng, 6), position), (blocks,), jnp.float32, low / len(cuts), largest / len(cuts))
        return jnp.repeat(jnp.exp(heights), dims[position] // blocks).reshape((-1,) + (1,) * (len(dims) - position - 1))

    loudness = one(*cuts[0])
    for cut in cuts[1:]:
        loudness = loudness * one(*cut)
    return loudness


def centred(rng, extent, scale, most, shards=(), kind=jnp.bfloat16):
    entries = scale * jax.random.normal(rng, extent, jnp.float32)
    if shards:
        entries = entries * shard_levels(rng, extent, shards, -0.22, 0.18)
    return jnp.clip(entries, -most, most).astype(kind)


def setup_inputs(seed: int = 0) -> dict:
    arg_keys = jax.random.split(jax.random.key(seed), 6)
    return {
        "features": centred(arg_keys[0], (LAYERS, SPLATS, F), 1.0, 4.0, ((0, 4), (1, 8))),
        "logits": draw_logits(jax.random.fold_in(arg_keys[5], 71), 0),
        "geometry": draw_geometry(jax.random.fold_in(arg_keys[5], 71), 0),
        "dest_slot": draw_dest_slot(jax.random.fold_in(arg_keys[5], 71), 0),
        "target": centred(arg_keys[4], (VIEWS, TILES, F, P_SIZE), 0.5, 3.0, ((1, 8),)),
    }


clamp_top = 0.99
feature_rate = 0.5
opacity_rate = 0.5


def pixel_places():
    places = jnp.arange(P_SIZE, dtype=jnp.int32)
    across = (places % W).astype(jnp.float32) + 0.5
    downward = (places // W).astype(jnp.float32) + 0.5
    return across, downward


def splat_fields(shapes):
    across, downward = pixel_places()
    delta_x = across[None, :] - shapes[0][:, None]
    delta_y = downward[None, :] - shapes[1][:, None]
    coef_a = jnp.exp(shapes[2])[:, None]
    coef_c = jnp.exp(shapes[3])[:, None]
    spread = jnp.exp(0.5 * (shapes[2] + shapes[3]))[:, None]
    coef_b = shapes[4][:, None] * spread
    quadric = coef_a * delta_x * delta_x + 2.0 * coef_b * delta_x * delta_y + coef_c * delta_y * delta_y
    falloff = jnp.exp(-0.5 * quadric)
    opacity = shapes[5][:, None]
    product = opacity * falloff
    coverage = jnp.minimum(product, clamp_top)
    return delta_x, delta_y, coef_a, coef_b, coef_c, spread, falloff, opacity, product, coverage


def layer_forward(inputs):
    slot_feats, shapes = inputs
    coverage = splat_fields(shapes)[9]
    log_keep = jnp.log(1.0 - coverage)
    before = jnp.cumsum(log_keep, axis=0) - log_keep
    weights = (coverage * jnp.exp(before)).astype(jnp.bfloat16)
    composite = jnp.dot(slot_feats.T, weights, preferred_element_type=jnp.float32)
    layer_keep = jnp.exp(jnp.sum(log_keep, axis=0))
    return composite, layer_keep


def layer_backward(inputs):
    slot_feats, shapes, grad_comp, grad_keep = inputs
    delta_x, delta_y, coef_a, coef_b, coef_c, spread, falloff, opacity, product, coverage = splat_fields(shapes)
    log_keep = jnp.log(1.0 - coverage)
    before = jnp.cumsum(log_keep, axis=0) - log_keep
    decayed = jnp.exp(before)
    exact_weight = coverage * decayed
    weights = exact_weight.astype(jnp.bfloat16)
    layer_keep = jnp.exp(jnp.sum(log_keep, axis=0))
    grad_feat = jnp.dot(weights, grad_comp.T, preferred_element_type=jnp.float32)
    grad_weight = jnp.dot(slot_feats, grad_comp, preferred_element_type=jnp.float32)
    grad_before = grad_weight * exact_weight
    later = jnp.sum(grad_before, axis=0)[None, :] - jnp.cumsum(grad_before, axis=0)
    grad_log = later + (grad_keep * layer_keep)[None, :]
    grad_coverage = grad_weight * decayed - grad_log / (1.0 - coverage)
    grad_product = jnp.where(product < clamp_top, grad_coverage, 0.0)
    grad_quadric = -0.5 * opacity * falloff * grad_product
    grad_mean_x = -2.0 * jnp.sum(grad_quadric * (coef_a * delta_x + coef_b * delta_y), axis=1)
    grad_mean_y = -2.0 * jnp.sum(grad_quadric * (coef_b * delta_x + coef_c * delta_y), axis=1)
    grad_first = jnp.sum(grad_quadric * delta_x * delta_x, axis=1)
    grad_cross = jnp.sum(grad_quadric * 2.0 * delta_x * delta_y, axis=1)
    grad_second = jnp.sum(grad_quadric * delta_y * delta_y, axis=1)
    grad_log_a = coef_a[:, 0] * grad_first + 0.5 * coef_b[:, 0] * grad_cross
    grad_log_c = coef_c[:, 0] * grad_second + 0.5 * coef_b[:, 0] * grad_cross
    grad_corr = spread[:, 0] * grad_cross
    opacity_flat = opacity[:, 0]
    grad_logit = opacity_flat * (1.0 - opacity_flat) * jnp.sum(falloff * grad_product, axis=1)
    grad_shape = jnp.stack([grad_mean_x, grad_mean_y, grad_log_a, grad_log_c, grad_corr, grad_logit])
    return grad_feat, grad_shape


def pick_rows(source_rows, chosen):
    return source_rows[chosen]


def pick_columns(source_rows, chosen):
    return source_rows[:, chosen]


def reference(features, logits, geometry, dest_slot, target):
    slot_total = TILES * S
    splat_feats = features
    logit_now = logits
    images = []
    shape_grads = []
    splat_ids = jnp.arange(SPLATS, dtype=jnp.int32)
    for view_index in range(VIEWS):
        slot_ids = dest_slot[view_index]
        holder = jnp.where(slot_ids >= 0, slot_ids, slot_total).astype(jnp.int32)
        owner_of = jax.vmap(lambda target_row: jnp.full((slot_total,), -1, jnp.int32).at[target_row].set(splat_ids, mode="drop"))(holder)
        filled = owner_of >= 0
        picks = jnp.maximum(owner_of, 0).astype(jnp.int32)
        slot_feats = jax.vmap(pick_rows)(splat_feats, picks)
        slot_feats = jnp.where(filled[:, :, None], slot_feats, jnp.zeros_like(slot_feats))
        opacity = jax.nn.sigmoid(logit_now)
        shape_source = jnp.concatenate([geometry[view_index], opacity[:, None, :]], axis=1)
        slot_shapes = jax.vmap(pick_columns)(shape_source, picks)
        slot_shapes = jnp.where(filled[:, None, :], slot_shapes, jnp.zeros_like(slot_shapes))
        tile_feats = slot_feats.reshape(LAYERS * TILES, S, F)
        tile_shapes = slot_shapes.reshape(LAYERS, 6, TILES, S).transpose(0, 2, 1, 3).reshape(LAYERS * TILES, 6, S)
        composites, layer_keeps = lax.map(layer_forward, (tile_feats, tile_shapes))
        composites = composites.reshape(LAYERS, TILES, F, P_SIZE)
        layer_keeps = layer_keeps.reshape(LAYERS, TILES, P_SIZE)
        ahead = jnp.concatenate([jnp.ones((1, TILES, P_SIZE), jnp.float32), jnp.cumprod(layer_keeps, axis=0)[:-1]], axis=0)
        summed = jnp.sum(ahead[:, :, None, :] * composites, axis=0)
        images.append(summed.astype(jnp.bfloat16))
        residual = summed - target[view_index].astype(jnp.float32)
        pixel_terms = jnp.sum(residual[None] * composites, axis=2)

        def rear_step(carried, pair):
            keep_here, term_here = pair
            return term_here + keep_here * carried, carried

        _, behind_flipped = lax.scan(rear_step, jnp.zeros((TILES, P_SIZE), jnp.float32), (layer_keeps[::-1], pixel_terms[::-1]))
        behind = behind_flipped[::-1]
        grad_keep = ahead * behind
        grad_comp = (ahead[:, :, None, :] * residual[None]).astype(jnp.bfloat16)
        grad_feat, grad_shape = lax.map(layer_backward, (tile_feats, tile_shapes, grad_comp.reshape(LAYERS * TILES, F, P_SIZE), grad_keep.reshape(LAYERS * TILES, P_SIZE)))
        grad_feat = grad_feat.reshape(LAYERS, slot_total, F)
        grad_shape = grad_shape.reshape(LAYERS, TILES, 6, S).transpose(0, 2, 1, 3).reshape(LAYERS, 6, slot_total)
        visible = slot_ids >= 0
        fetched = jnp.where(visible, slot_ids, 0).astype(jnp.int32)
        splat_grad_feat = jax.vmap(pick_rows)(grad_feat, fetched)
        splat_grad_feat = jnp.where(visible[:, :, None], splat_grad_feat, jnp.zeros_like(splat_grad_feat))
        splat_grad_shape = jax.vmap(pick_columns)(grad_shape, fetched)
        splat_grad_shape = jnp.where(visible[:, None, :], splat_grad_shape, jnp.zeros_like(splat_grad_shape))
        shape_grads.append(splat_grad_shape[:, :5])
        splat_feats = (splat_feats.astype(jnp.float32) - feature_rate * splat_grad_feat).astype(jnp.bfloat16)
        logit_now = logit_now - opacity_rate * splat_grad_shape[:, 5]
    return jnp.stack(images), splat_feats, logit_now, jnp.stack(shape_grads)
```

```python
import functools

import jax
import jax.numpy as jnp
from jax import lax
from jax.experimental import pallas as pl
from jax.experimental.pallas import tpu as pltpu
from jax.sharding import PartitionSpec as P

W = 32
S = 128
clamp_top = 0.99
feature_rate = 0.5
opacity_rate = 0.5
f32 = jnp.float32
bf16 = jnp.bfloat16


def dot(lhs, rhs, left=1, right=0):
    return lax.dot_general(
        lhs, rhs, (((left,), (right,)), ((), ())), preferred_element_type=f32
    )


def three_parts(value):
    high = value.astype(bf16).astype(f32)
    rest = value - high
    mid = rest.astype(bf16).astype(f32)
    return high, mid, rest - mid


def two_parts(value):
    high = value.astype(bf16)
    low = (value - high.astype(f32)).astype(bf16)
    return jnp.concatenate([high, low], axis=1)


def iota(shape, axis):
    return lax.broadcasted_iota(jnp.int32, shape, axis)


def put_rows(rows, shape):
    place = iota(shape, 0)
    total = jnp.zeros(shape, f32)
    for at, row in enumerate(rows):
        total = jnp.where(place == at, row, total)
    return total


def splat_kernel(
    owners, layers, views, tiles, share,
    feat_ref, logit_ref, geom_ref, dest_ref, target_ref,
    img_ref, newf_ref, newl_ref, sg_ref,
    pay, got, back, ret, gath_f, gath_s, part_f, part_s, in_f, in_s,
    perm, place_t, places, tri, tril, ones2,
    fall_s, dec_s, w_s, comp_s, keep_s, ahead_s, gk_s, res_s, run_s,
    cur_f, cur_l,
    a_send, a_recv, gf_send, gf_recv, gs_send, gs_recv,
    pf_send, pf_recv, ps_send, ps_recv, b_send, b_recv,
):
    me_t = lax.axis_index("tile")
    me_d = lax.axis_index("depth")
    owned, feats = feat_ref.shape
    cap = owned // owners
    wire = pay.dtype

    def tile_peer(k):
        return lax.rem(me_t + k, owners)

    def depth_peer(k):
        return lax.rem(me_d + k, layers)

    barrier = pltpu.get_barrier_semaphore()
    for k in range(1, owners):
        pl.semaphore_signal(barrier, inc=1, device_id=(tile_peer(k), me_d), device_id_type=pl.DeviceIdType.MESH)
    for k in range(1, layers):
        pl.semaphore_signal(barrier, inc=1, device_id=(me_t, depth_peer(k)), device_id_type=pl.DeviceIdType.MESH)

    pixel = iota((share, S), 0) + me_d * share
    places[0] = (pixel & (W - 1)).astype(f32) + 0.5
    places[1] = (pixel >> (W.bit_length() - 1)).astype(f32) + 0.5
    row = iota((S, S), 0)
    col = iota((S, S), 1)
    earlier = (row < col).astype(f32).astype(bf16)
    later_mat = (row > col).astype(f32).astype(bf16)
    ones = jnp.ones((S, S), bf16)
    half = jnp.concatenate([earlier, ones], axis=1)
    tri[...] = jnp.concatenate([half, half], axis=0)
    tril[...] = jnp.concatenate([later_mat, later_mat], axis=0)
    ones2[...] = jnp.ones((2 * feats, feats), bf16)
    cur_f[...] = feat_ref[...]
    cur_l[...] = logit_ref[...]

    pl.semaphore_wait(barrier, owners + layers - 2)

    def tile_copy(v, k, src, dst, send, recv):
        return pltpu.make_async_remote_copy(
            src_ref=src.at[v, tile_peer(k)], dst_ref=dst.at[v, me_t],
            send_sem=send.at[v, k], recv_sem=recv.at[v, k],
            device_id=(tile_peer(k), me_d), device_id_type=pl.DeviceIdType.MESH,
        )

    def exchange(v, src, dst, send, recv):
        for k in range(1, owners):
            tile_copy(v, k, src, dst, send, recv).start()
        dst[v, me_t] = src[v, me_t]
        for k in range(1, owners):
            tile_copy(v, k, src, dst, send, recv).wait()

    def depth_copy(v, k, src, dst, src_at, send, recv):
        return pltpu.make_async_remote_copy(
            src_ref=src.at[v, src_at], dst_ref=dst.at[v, me_d],
            send_sem=send.at[v, k], recv_sem=recv.at[v, k],
            device_id=(me_t, depth_peer(k)), device_id_type=pl.DeviceIdType.MESH,
        )

    def slot_rows(v, e, t):
        g = gath_s[v, e, :, t * S : (t + 1) * S]
        coef_a = jnp.exp(g[2:3])
        coef_c = jnp.exp(g[3:4])
        spread = jnp.exp(0.5 * (g[2:3] + g[3:4]))
        return g[0:1], g[1:2], coef_a, g[4:5] * spread, coef_c, spread, g[5:6]

    def forward(v, e):
        for t in range(tiles):
            g0, g1, ca, cb, cc, _, opacity = slot_rows(v, e, t)
            dx = places[0] - g0
            dy = places[1] - g1
            quadric = ca * dx * dx + 2.0 * cb * dx * dy + cc * dy * dy
            fall = jnp.exp(-0.5 * quadric)
            coverage = jnp.minimum(opacity * fall, clamp_top)
            log_keep = jnp.log(1.0 - coverage)
            sums = dot(two_parts(log_keep), tri[...])
            decayed = jnp.exp(sums[:, :S])
            weights = (coverage * decayed).astype(bf16)
            fall_s[e, t] = fall
            dec_s[e, t] = decayed
            w_s[e, t] = weights
            keep_s[e, t] = jnp.exp(sums[:, S:])
            comp_s[e, t] = dot(weights, gath_f[v, e, t * S : (t + 1) * S, :])

    def combine(v):
        for t in range(tiles):
            res_s[t] = jnp.zeros((share, feats), f32)
            run_s[...] = jnp.ones((share, feats), f32)

            def front(e, carry):
                ahead = run_s[...]
                ahead_s[e, t] = ahead
                res_s[t] = res_s[t] + ahead * comp_s[e, t]
                run_s[...] = ahead * keep_s[e, t]
                return carry

            lax.fori_loop(0, layers, front, 0)
            summed = res_s[t]
            img_ref[v, t] = summed.astype(bf16)
            res_s[t] = summed - target_ref[v, t].astype(f32)
            run_s[...] = jnp.zeros((share, feats), f32)

            def rear(i, carry):
                e = layers - 1 - i
                behind = run_s[...]
                keep = keep_s[e, t]
                gk_s[e, t] = ahead_s[e, t] * behind * keep
                terms = dot(two_parts(res_s[t] * comp_s[e, t]), ones2[...])
                run_s[...] = terms + keep * behind
                return carry

            lax.fori_loop(0, layers, rear, 0)

    def backward(v, e):
        for t in range(tiles):
            g0, g1, ca, cb, cc, spread, opacity = slot_rows(v, e, t)
            grad_comp = (ahead_s[e, t] * res_s[t]).astype(bf16)
            span = slice(t * S, (t + 1) * S)
            part_f[v, e, span, :] = dot(w_s[e, t], grad_comp, 0, 0).astype(bf16)
            grad_weight = dot(grad_comp, gath_f[v, e, span, :], 1, 1)
            decayed = dec_s[e, t]
            fall = fall_s[e, t]
            product = opacity * fall
            coverage = jnp.minimum(product, clamp_top)
            grad_decayed = grad_weight * decayed
            later = dot(two_parts(grad_decayed * coverage), tril[...])
            grad_log = later + gk_s[e, t]
            grad_coverage = grad_decayed - grad_log / (1.0 - coverage)
            moment = fall * jnp.where(product < clamp_top, grad_coverage, 0.0)
            dx = places[0] - g0
            dy = places[1] - g1
            moment_x = moment * dx
            moment_y = moment * dy

            def total(value):
                return jnp.sum(value, axis=0, keepdims=True)

            m0 = total(moment)
            mx = opacity * total(moment_x)
            my = opacity * total(moment_y)
            first = -0.5 * opacity * total(moment_x * dx)
            cross = -1.0 * opacity * total(moment_x * dy)
            second = -0.5 * opacity * total(moment_y * dy)
            part_s[v, e, :, span] = put_rows(
                [
                    ca * mx + cb * my,
                    cb * mx + cc * my,
                    ca * first + 0.5 * cb * cross,
                    cc * second + 0.5 * cb * cross,
                    spread * cross,
                    opacity * (1.0 - opacity) * m0,
                ],
                (8, S),
            )

    def aux_rows(eight):
        high, mid, low = three_parts(eight)
        zero = jnp.zeros((feats - 24, owned), f32)
        return jnp.concatenate([high, mid, low, zero], axis=0).astype(bf16)

    def pack(ref, v, value):
        ref[v] = value.reshape(owners, cap, value.shape[1]).astype(wire)

    def unpack(ref, v):
        return ref[v].astype(f32).reshape(owners * cap, 2 * feats)

    for v in range(views):
        dest = dest_ref[v]
        low_edge = iota((owners, owned), 0) * owned
        hit = (dest >= low_edge) & (dest < low_edge + owned)
        matches = hit.astype(f32)
        upper = (iota((owned, owned), 0) < iota((owned, owned), 1)).astype(f32).astype(bf16)
        rank = dot(matches.astype(bf16), upper)
        count = iota((owners, owned), 0).astype(f32) * cap + rank + 1.0
        position = jnp.sum(matches * count, axis=0, keepdims=True) - 1.0
        slot_id = jnp.sum(
            matches * (dest - low_edge + 1).astype(f32), axis=0, keepdims=True
        )
        perm_now = (iota((owned, owned), 0).astype(f32) == position).astype(f32).astype(bf16)
        perm[v] = perm_now
        logit = cur_l[...]
        opacity = 1.0 / (1.0 + jnp.exp(-logit))
        rows8 = iota((8, owned), 0)
        eight = jnp.where(rows8 == 5, opacity, jnp.where(rows8 == 6, slot_id, geom_ref[v]))
        pack(
            pay, v,
            jnp.concatenate(
                [dot(perm_now, cur_f[...]), dot(perm_now, aux_rows(eight), 1, 1)], axis=1
            ),
        )
        exchange(v, pay, got, a_send, a_recv)

        arrived = unpack(got, v)
        aux = arrived[:, feats:]
        aux_t = aux.T
        to_slot = (iota((owned, owned), 0).astype(f32) + 1.0 == aux_t[6:7, :]).astype(f32).astype(bf16)
        place_t[v] = (iota((owned, owned), 1).astype(f32) + 1.0 == aux[:, 6:7]).astype(f32).astype(bf16)
        gath_f[v, me_d] = dot(to_slot, arrived[:, :feats].astype(bf16)).astype(bf16)
        shapes = dot(aux_t[0:32].astype(bf16), to_slot, 1, 1)
        gath_s[v, me_d] = shapes[0:8] + shapes[8:16] + shapes[16:24]
        for k in range(1, layers):
            depth_copy(v, k, gath_f, gath_f, me_d, gf_send, gf_recv).start()
            depth_copy(v, k, gath_s, gath_s, me_d, gs_send, gs_recv).start()
        forward(v, me_d)

        def fwd_step(k, carry):
            depth_copy(v, k, gath_f, gath_f, me_d, gf_send, gf_recv).wait()
            depth_copy(v, k, gath_s, gath_s, me_d, gs_send, gs_recv).wait()
            forward(v, lax.rem(me_d + layers - k, layers))
            return carry

        lax.fori_loop(1, layers, fwd_step, 0)
        combine(v)

        def bwd_step(k, carry):
            e = depth_peer(k)
            backward(v, e)
            depth_copy(v, k, part_f, in_f, e, pf_send, pf_recv).start()
            depth_copy(v, k, part_s, in_s, e, ps_send, ps_recv).start()
            return carry

        lax.fori_loop(1, layers, bwd_step, 0)
        backward(v, me_d)
        sum_f = part_f[v, me_d].astype(f32)
        sum_s = part_s[v, me_d]
        for k in range(1, layers):
            e = depth_peer(k)
            depth_copy(v, k, part_f, in_f, e, pf_send, pf_recv).wait()
            depth_copy(v, k, part_s, in_s, e, ps_send, ps_recv).wait()
            origin = lax.rem(me_d + layers - k, layers)
            sum_f = sum_f + in_f[v, origin].astype(f32)
            sum_s = sum_s + in_s[v, origin]
        pack(
            back, v,
            jnp.concatenate(
                [
                    dot(place_t[v], sum_f.astype(bf16)),
                    dot(place_t[v], aux_rows(sum_s), 1, 1),
                ],
                axis=1,
            ),
        )
        exchange(v, back, ret, b_send, b_recv)
        returned = unpack(ret, v).astype(bf16)
        grad_feat = dot(perm[v], returned[:, :feats], 0, 0)
        grad_rows = dot(returned[:, feats:], perm[v], 0, 0)
        grad_eight = grad_rows[0:8] + grad_rows[8:16] + grad_rows[16:24]
        sg_ref[v] = grad_eight
        cur_f[...] = (cur_f[...].astype(f32) - feature_rate * grad_feat).astype(bf16)
        cur_l[...] = cur_l[...] - opacity_rate * grad_eight[5:6]

    newf_ref[...] = cur_f[...]
    newl_ref[...] = cur_l[...]


def body(features, logits, geometry, dest_slot, target):
    owners = lax.axis_size("tile")
    layers = lax.axis_size("depth")
    depth_here = lax.axis_index("depth")
    views, tiles, feats, pixels = target.shape
    owned = features.shape[1]
    cap = owned // owners
    share = pixels // layers
    wire = bf16 if cap % 16 == 0 else f32
    own_target = lax.dynamic_slice_in_dim(target, depth_here * share, share, 3)
    own_target = own_target.transpose(0, 1, 3, 2)
    geom = jnp.pad(geometry[:, 0], ((0, 0), (0, 3), (0, 0)))
    vm = pl.BlockSpec(memory_space=pltpu.VMEM)
    grid = (layers, tiles, share, S)
    dma = pltpu.SemaphoreType.DMA
    images, new_f, new_l, grads = pl.pallas_call(
        functools.partial(splat_kernel, owners, layers, views, tiles, share),
        out_shape=(
            jax.ShapeDtypeStruct((views, tiles, share, feats), bf16),
            jax.ShapeDtypeStruct((owned, feats), bf16),
            jax.ShapeDtypeStruct((1, owned), f32),
            jax.ShapeDtypeStruct((views, 8, owned), f32),
        ),
        in_specs=[vm] * 5,
        out_specs=(vm,) * 4,
        scratch_shapes=[
            pltpu.VMEM((views, owners, cap, 2 * feats), wire),
            pltpu.VMEM((views, owners, cap, 2 * feats), wire),
            pltpu.VMEM((views, owners, cap, 2 * feats), wire),
            pltpu.VMEM((views, owners, cap, 2 * feats), wire),
            pltpu.VMEM((views, layers, owned, feats), bf16),
            pltpu.VMEM((views, layers, 8, owned), f32),
            pltpu.VMEM((views, layers, owned, feats), bf16),
            pltpu.VMEM((views, layers, 8, owned), f32),
            pltpu.VMEM((views, layers, owned, feats), bf16),
            pltpu.VMEM((views, layers, 8, owned), f32),
            pltpu.VMEM((views, owned, owned), bf16),
            pltpu.VMEM((views, owned, owned), bf16),
            pltpu.VMEM((2, share, S), f32),
            pltpu.VMEM((2 * S, 2 * S), bf16),
            pltpu.VMEM((2 * S, S), bf16),
            pltpu.VMEM((2 * feats, feats), bf16),
            pltpu.VMEM(grid, f32),
            pltpu.VMEM(grid, f32),
            pltpu.VMEM(grid, bf16),
            pltpu.VMEM(grid, f32),
            pltpu.VMEM(grid, f32),
            pltpu.VMEM(grid, f32),
            pltpu.VMEM(grid, f32),
            pltpu.VMEM((tiles, share, feats), f32),
            pltpu.VMEM((share, feats), f32),
            pltpu.VMEM((owned, feats), bf16),
            pltpu.VMEM((1, owned), f32),
            dma((views, owners)), dma((views, owners)),
            dma((views, layers)), dma((views, layers)),
            dma((views, layers)), dma((views, layers)),
            dma((views, layers)), dma((views, layers)),
            dma((views, layers)), dma((views, layers)),
            dma((views, owners)), dma((views, owners)),
        ],
        compiler_params=pltpu.CompilerParams(
            collective_id=0, has_side_effects=True, vmem_limit_bytes=56 * 1024 * 1024
        ),
        name="splat_views",
    )(features[0], logits, geom, dest_slot, own_target)
    return (
        images.transpose(0, 1, 3, 2),
        new_f[None],
        new_l,
        grads[:, None, :5, :],
    )


def solution(mesh):
    placed = (
        P("depth", "tile", None),
        P("depth", "tile"),
        P(None, "depth", None, "tile"),
        P(None, "depth", "tile"),
        P(None, "tile", None, None),
    )
    return jax.shard_map(
        body,
        mesh=mesh,
        in_specs=placed,
        out_specs=(
            P(None, "tile", None, "depth"),
            P("depth", "tile", None),
            P("depth", "tile"),
            P(None, "depth", None, "tile"),
        ),
        check_vma=False,
    )
```

```python
import functools

import jax
import jax.numpy as jnp
from jax import lax
from jax.experimental import pallas as pl
from jax.experimental.pallas import tpu as pltpu
from jax.sharding import PartitionSpec as P

W = 32
S = 128
clamp_top = 0.99
feature_rate = 0.5
opacity_rate = 0.5
f32 = jnp.float32
bf16 = jnp.bfloat16


def dot(lhs, rhs, left=1, right=0):
    return lax.dot_general(
        lhs, rhs, (((left,), (right,)), ((), ())), preferred_element_type=f32
    )


def three_parts(value):
    high = value.astype(bf16).astype(f32)
    rest = value - high
    mid = rest.astype(bf16).astype(f32)
    return high, mid, rest - mid


def two_parts(value):
    high = value.astype(bf16)
    low = (value - high.astype(f32)).astype(bf16)
    return jnp.concatenate([high, low], axis=1)


def iota(shape, axis):
    return lax.broadcasted_iota(jnp.int32, shape, axis)


def put_rows(rows, shape):
    place = iota(shape, 0)
    total = jnp.zeros(shape, f32)
    for at, row in enumerate(rows):
        total = jnp.where(place == at, row, total)
    return total


def splat_kernel(
    owners, layers, views, tiles, share,
    feat_ref, logit_ref, geom_ref, dest_ref, target_ref,
    img_ref, newf_ref, newl_ref, sg_ref,
    pay, got, back, ret, mine_f, mine_s, gath_f, gath_s, part_f, part_s, in_f, in_s,
    img_out, img_in, perm, ids, place_t, places, tri, tril, ones2,
    fall_s, dec_s, w_s, comp_s, keep_s, ahead_s, gk_s, res_s, run_s,
    cur_f, cur_l,
    a_send, a_recv, gf_send, gf_recv, gs_send, gs_recv,
    pf_send, pf_recv, ps_send, ps_recv, b_send, b_recv, i_send, i_recv,
):
    me_t = lax.axis_index("tile")
    me_d = lax.axis_index("depth")
    owned, feats = feat_ref.shape
    cap = owned // owners
    wire = pay.dtype
    group = layers // tiles
    pixels = tiles * share
    my_tile = me_d // group
    partner = lax.rem(me_d + group, layers)

    def tile_peer(k):
        return lax.rem(me_t + k, owners)

    def depth_peer(k):
        return lax.rem(me_d + k, layers)

    barrier = pltpu.get_barrier_semaphore()
    for k in range(1, owners):
        pl.semaphore_signal(barrier, inc=1, device_id=(tile_peer(k), me_d), device_id_type=pl.DeviceIdType.MESH)
    for k in range(1, layers):
        pl.semaphore_signal(barrier, inc=1, device_id=(me_t, depth_peer(k)), device_id_type=pl.DeviceIdType.MESH)

    lane_row = iota((pixels, S), 0)
    pixel = lane_row + jnp.where(lane_row < share, me_d, partner - 1) * share
    places[0] = (pixel & (W - 1)).astype(f32) + 0.5
    places[1] = (pixel >> (W.bit_length() - 1)).astype(f32) + 0.5
    row = iota((S, S), 0)
    col = iota((S, S), 1)
    earlier = (row < col).astype(f32).astype(bf16)
    later_mat = (row > col).astype(f32).astype(bf16)
    ones = jnp.ones((S, S), bf16)
    half = jnp.concatenate([earlier, ones], axis=1)
    tri[...] = jnp.concatenate([half, half], axis=0)
    tril[...] = jnp.concatenate([later_mat, later_mat], axis=0)
    ones2[...] = jnp.ones((2 * feats, feats), bf16)
    cur_f[...] = feat_ref[...]
    cur_l[...] = logit_ref[...]

    def tile_copy(v, k, src, dst, send, recv):
        return pltpu.make_async_remote_copy(
            src_ref=src.at[v, tile_peer(k)], dst_ref=dst.at[v, me_t],
            send_sem=send.at[v, k], recv_sem=recv.at[v, k],
            device_id=(tile_peer(k), me_d), device_id_type=pl.DeviceIdType.MESH,
        )

    def exchange(v, src, dst, send, recv, beside=None):
        for k in range(1, owners):
            tile_copy(v, k, src, dst, send, recv).start()
        dst[v, me_t] = src[v, me_t]
        if beside is not None:
            beside()
        for k in range(1, owners):
            tile_copy(v, k, src, dst, send, recv).wait()

    def depth_copy(v, k, src, dst, src_at, send, recv):
        return pltpu.make_async_remote_copy(
            src_ref=src.at[v, src_at], dst_ref=dst.at[v, me_d],
            send_sem=send.at[v, k], recv_sem=recv.at[v, k],
            device_id=(me_t, depth_peer(k)), device_id_type=pl.DeviceIdType.MESH,
        )

    def image_copy(v):
        return pltpu.make_async_remote_copy(
            src_ref=img_out.at[v], dst_ref=img_in.at[v],
            send_sem=i_send.at[v], recv_sem=i_recv.at[v],
            device_id=(me_t, partner), device_id_type=pl.DeviceIdType.MESH,
        )

    def slot_rows(v, e):
        g = gath_s[v, e]
        coef_a = jnp.exp(g[2:3])
        coef_c = jnp.exp(g[3:4])
        spread = jnp.exp(0.5 * (g[2:3] + g[3:4]))
        return g[0:1], g[1:2], coef_a, g[4:5] * spread, coef_c, spread, g[5:6]

    def forward(v, e):
        g0, g1, ca, cb, cc, _, opacity = slot_rows(v, e)
        dx = places[0] - g0
        dy = places[1] - g1
        quadric = ca * dx * dx + 2.0 * cb * dx * dy + cc * dy * dy
        fall = jnp.exp(-0.5 * quadric)
        coverage = jnp.minimum(opacity * fall, clamp_top)
        log_keep = jnp.log(1.0 - coverage)
        sums = dot(two_parts(log_keep), tri[...])
        decayed = jnp.exp(sums[:, :S])
        weights = (coverage * decayed).astype(bf16)
        fall_s[e] = fall
        dec_s[e] = decayed
        w_s[e] = weights
        keep_s[e] = jnp.exp(sums[:, S:])
        comp_s[e] = dot(weights, gath_f[v, e])

    def combine(v):
        res_s[...] = jnp.zeros((pixels, feats), f32)
        run_s[...] = jnp.ones((pixels, feats), f32)

        def front(e, carry):
            ahead = run_s[...]
            ahead_s[e] = ahead
            res_s[...] = res_s[...] + ahead * comp_s[e]
            run_s[...] = ahead * keep_s[e]
            return carry

        lax.fori_loop(0, layers, front, 0)
        summed = res_s[...]
        img_ref[v, my_tile] = summed[:share].T.astype(bf16)
        img_out[v] = summed[share:].T.astype(bf16)
        res_s[...] = summed - target_ref[v].astype(f32)
        run_s[...] = jnp.zeros((pixels, feats), f32)

        def rear(i, carry):
            e = layers - 1 - i
            behind = run_s[...]
            keep = keep_s[e]
            gk_s[e] = ahead_s[e] * behind * keep
            terms = dot(two_parts(res_s[...] * comp_s[e]), ones2[...])
            run_s[...] = terms + keep * behind
            return carry

        lax.fori_loop(0, layers, rear, 0)

    def backward(v, e, out_f, out_s):
        g0, g1, ca, cb, cc, spread, opacity = slot_rows(v, e)
        grad_comp = (ahead_s[e] * res_s[...]).astype(bf16)
        out_f[v, e] = dot(w_s[e], grad_comp, 0, 0).astype(bf16)
        grad_weight = dot(grad_comp, gath_f[v, e], 1, 1)
        decayed = dec_s[e]
        fall = fall_s[e]
        product = opacity * fall
        coverage = jnp.minimum(product, clamp_top)
        grad_decayed = grad_weight * decayed
        later = dot(two_parts(grad_decayed * coverage), tril[...])
        grad_log = later + gk_s[e]
        grad_coverage = grad_decayed - grad_log / (1.0 - coverage)
        moment = fall * jnp.where(product < clamp_top, grad_coverage, 0.0)
        dx = places[0] - g0
        dy = places[1] - g1
        moment_x = moment * dx
        moment_y = moment * dy

        def total(value):
            return jnp.sum(value, axis=0, keepdims=True)

        m0 = total(moment)
        mx = opacity * total(moment_x)
        my = opacity * total(moment_y)
        first = -0.5 * opacity * total(moment_x * dx)
        cross = -1.0 * opacity * total(moment_x * dy)
        second = -0.5 * opacity * total(moment_y * dy)
        out_s[v, e] = put_rows(
            [
                ca * mx + cb * my,
                cb * mx + cc * my,
                ca * first + 0.5 * cb * cross,
                cc * second + 0.5 * cb * cross,
                spread * cross,
                opacity * (1.0 - opacity) * m0,
            ],
            (8, S),
        )

    def aux_rows(eight):
        high, mid, low = three_parts(eight)
        zero = jnp.zeros((feats - 24, owned), f32)
        return jnp.concatenate([high, mid, low, zero], axis=0).astype(bf16)

    def pack(ref, v, value):
        ref[v] = value.reshape(owners, cap, value.shape[1]).astype(wire)

    def unpack(ref, v):
        return ref[v].astype(f32).reshape(owners * cap, 2 * feats)

    def indices(v):
        dest = dest_ref[v]
        low_edge = iota((owners, owned), 0) * owned
        hit = (dest >= low_edge) & (dest < low_edge + owned)
        matches = hit.astype(f32)
        upper = (iota((owned, owned), 0) < iota((owned, owned), 1)).astype(f32).astype(bf16)
        rank = dot(matches.astype(bf16), upper)
        count = iota((owners, owned), 0).astype(f32) * cap + rank + 1.0
        position = jnp.sum(matches * count, axis=0, keepdims=True) - 1.0
        ids[v] = jnp.sum(
            matches * (dest - low_edge + 1).astype(f32), axis=0, keepdims=True
        )
        perm[v] = (iota((owned, owned), 0).astype(f32) == position).astype(f32).astype(bf16)

    def dispatch(v):
        opacity = 1.0 / (1.0 + jnp.exp(-cur_l[...]))
        rows8 = iota((8, owned), 0)
        eight = jnp.where(rows8 == 5, opacity, jnp.where(rows8 == 6, ids[v], geom_ref[v]))
        pack(
            pay, v,
            jnp.concatenate(
                [dot(perm[v], cur_f[...]), dot(perm[v], aux_rows(eight), 1, 1)], axis=1
            ),
        )

    def later_indices():
        for v in range(1, views):
            indices(v)

    indices(0)
    for v in range(views):
        dispatch(v)
        if v == 0:
            pl.semaphore_wait(barrier, owners + layers - 2)
        exchange(v, pay, got, a_send, a_recv, later_indices if v == 0 else None)

        arrived = unpack(got, v)
        aux = arrived[:, feats:]
        aux_t = aux.T
        to_slot = (iota((owned, owned), 0).astype(f32) + 1.0 == aux_t[6:7, :]).astype(f32).astype(bf16)
        place_t[v] = (iota((owned, owned), 1).astype(f32) + 1.0 == aux[:, 6:7]).astype(f32).astype(bf16)
        slot_f = dot(to_slot, arrived[:, :feats].astype(bf16)).astype(bf16)
        shapes = dot(aux_t[0:32].astype(bf16), to_slot, 1, 1)
        shapes = shapes[0:8] + shapes[8:16] + shapes[16:24]
        for t in range(tiles):
            mine_f[v, t] = slot_f[t * S : (t + 1) * S]
            mine_s[v, t] = shapes[:, t * S : (t + 1) * S]

        def gather(k):
            there = depth_peer(k) // group
            return (
                depth_copy(v, k, mine_f, gath_f, there, gf_send, gf_recv),
                depth_copy(v, k, mine_s, gath_s, there, gs_send, gs_recv),
            )

        for k in range(1, layers):
            for copy in gather(k):
                copy.start()
        gath_f[v, me_d] = mine_f[v, my_tile]
        gath_s[v, me_d] = mine_s[v, my_tile]
        forward(v, me_d)

        def fwd_step(k, carry):
            for copy in gather(k):
                copy.wait()
            forward(v, lax.rem(me_d + layers - k, layers))
            return carry

        lax.fori_loop(1, layers, fwd_step, 0)
        combine(v)

        def give(k):
            e = depth_peer(k)
            return (
                depth_copy(v, k, part_f, in_f, e, pf_send, pf_recv),
                depth_copy(v, k, part_s, in_s, e, ps_send, ps_recv),
            )

        def bwd_step(k, carry):
            backward(v, depth_peer(k), part_f, part_s)
            for copy in give(k):
                copy.start()
            return carry

        lax.fori_loop(1, layers, bwd_step, 0)
        backward(v, me_d, in_f, in_s)
        for k in range(1, layers):
            for copy in give(k):
                copy.wait()
        image_copy(v).start()
        sums_f = []
        sums_s = []
        for t in range(tiles):
            sums_f.append(sum(in_f[v, z].astype(f32) for z in range(t * group, (t + 1) * group)))
            sums_s.append(sum(in_s[v, z] for z in range(t * group, (t + 1) * group)))
        sum_f = jnp.concatenate(sums_f, axis=0)
        sum_s = jnp.concatenate(sums_s, axis=1)
        pack(
            back, v,
            jnp.concatenate(
                [
                    dot(place_t[v], sum_f.astype(bf16)),
                    dot(place_t[v], aux_rows(sum_s), 1, 1),
                ],
                axis=1,
            ),
        )
        exchange(v, back, ret, b_send, b_recv)
        returned = unpack(ret, v).astype(bf16)
        grad_feat = dot(perm[v], returned[:, :feats], 0, 0)
        grad_rows = dot(returned[:, feats:], perm[v], 0, 0)
        grad_eight = grad_rows[0:8] + grad_rows[8:16] + grad_rows[16:24]
        sg_ref[v] = grad_eight
        cur_f[...] = (cur_f[...].astype(f32) - feature_rate * grad_feat).astype(bf16)
        cur_l[...] = cur_l[...] - opacity_rate * grad_eight[5:6]

    for v in range(views):
        image_copy(v).wait()
        img_ref[v, 1 - my_tile] = img_in[v]
    newf_ref[...] = cur_f[...]
    newl_ref[...] = cur_l[...]


def body(features, logits, geometry, dest_slot, target):
    owners = lax.axis_size("tile")
    layers = lax.axis_size("depth")
    depth_here = lax.axis_index("depth")
    views, tiles, feats, pixels = target.shape
    owned = features.shape[1]
    cap = owned // owners
    share = pixels // layers
    wire = bf16 if cap % 16 == 0 else f32
    if tiles != 2 or layers % tiles or owned > 256:
        raise ValueError("unsupported split")
    group = layers // tiles
    tile_here = depth_here // group
    partner = lax.rem(depth_here + group, layers)
    own_target = jnp.concatenate(
        [
            lax.dynamic_slice(target, (0, tile_here, 0, place * share), (views, 1, feats, share))[:, 0]
            for place in (depth_here, partner)
        ],
        axis=2,
    ).transpose(0, 2, 1)
    geom = jnp.pad(geometry[:, 0], ((0, 0), (0, 3), (0, 0)))
    vm = pl.BlockSpec(memory_space=pltpu.VMEM)
    grid = (layers, tiles * share, S)
    dma = pltpu.SemaphoreType.DMA
    images, new_f, new_l, grads = pl.pallas_call(
        functools.partial(splat_kernel, owners, layers, views, tiles, share),
        out_shape=(
            jax.ShapeDtypeStruct((views, tiles, feats, share), bf16),
            jax.ShapeDtypeStruct((owned, feats), bf16),
            jax.ShapeDtypeStruct((1, owned), f32),
            jax.ShapeDtypeStruct((views, 8, owned), f32),
        ),
        in_specs=[vm] * 5,
        out_specs=(vm,) * 4,
        scratch_shapes=[
            pltpu.VMEM((views, owners, cap, 2 * feats), wire),
            pltpu.VMEM((views, owners, cap, 2 * feats), wire),
            pltpu.VMEM((views, owners, cap, 2 * feats), wire),
            pltpu.VMEM((views, owners, cap, 2 * feats), wire),
            pltpu.VMEM((views, tiles, S, feats), bf16),
            pltpu.VMEM((views, tiles, 8, S), f32),
            pltpu.VMEM((views, layers, S, feats), bf16),
            pltpu.VMEM((views, layers, 8, S), f32),
            pltpu.VMEM((views, layers, S, feats), bf16),
            pltpu.VMEM((views, layers, 8, S), f32),
            pltpu.VMEM((views, layers, S, feats), bf16),
            pltpu.VMEM((views, layers, 8, S), f32),
            pltpu.VMEM((views, feats, share), bf16),
            pltpu.VMEM((views, feats, share), bf16),
            pltpu.VMEM((views, owned, owned), bf16),
            pltpu.VMEM((views, 1, owned), f32),
            pltpu.VMEM((views, owned, owned), bf16),
            pltpu.VMEM((2, tiles * share, S), f32),
            pltpu.VMEM((2 * S, 2 * S), bf16),
            pltpu.VMEM((2 * S, S), bf16),
            pltpu.VMEM((2 * feats, feats), bf16),
            pltpu.VMEM(grid, f32),
            pltpu.VMEM(grid, f32),
            pltpu.VMEM(grid, bf16),
            pltpu.VMEM(grid, f32),
            pltpu.VMEM(grid, f32),
            pltpu.VMEM(grid, f32),
            pltpu.VMEM(grid, f32),
            pltpu.VMEM((tiles * share, feats), f32),
            pltpu.VMEM((tiles * share, feats), f32),
            pltpu.VMEM((owned, feats), bf16),
            pltpu.VMEM((1, owned), f32),
            dma((views, owners)), dma((views, owners)),
            dma((views, layers)), dma((views, layers)),
            dma((views, layers)), dma((views, layers)),
            dma((views, layers)), dma((views, layers)),
            dma((views, layers)), dma((views, layers)),
            dma((views, owners)), dma((views, owners)),
            dma((views,)), dma((views,)),
        ],
        compiler_params=pltpu.CompilerParams(
            collective_id=0, has_side_effects=True, vmem_limit_bytes=56 * 1024 * 1024
        ),
        name="splat_views",
    )(features[0], logits, geom, dest_slot, own_target)
    return (
        images,
        new_f[None],
        new_l,
        grads[:, None, :5, :],
    )


def solution(mesh):
    placed = (
        P("depth", "tile", None),
        P("depth", "tile"),
        P(None, "depth", None, "tile"),
        P(None, "depth", "tile"),
        P(None, "tile", None, None),
    )
    return jax.shard_map(
        body,
        mesh=mesh,
        in_specs=placed,
        out_specs=(
            P(None, "tile", None, "depth"),
            P("depth", "tile", None),
            P("depth", "tile"),
            P(None, "depth", None, "tile"),
        ),
        check_vma=False,
    )
```

```python
import functools

import jax
import jax.numpy as jnp
from jax import lax
from jax.experimental import pallas as pl
from jax.experimental.pallas import tpu as pltpu
from jax.sharding import PartitionSpec as P

W = 32
S = 128
clamp_top = 0.99
feature_rate = 0.5
opacity_rate = 0.5
f32 = jnp.float32
bf16 = jnp.bfloat16


def dot(lhs, rhs, left=1, right=0):
    return lax.dot_general(
        lhs, rhs, (((left,), (right,)), ((), ())), preferred_element_type=f32
    )


def three_parts(value):
    high = value.astype(bf16).astype(f32)
    rest = value - high
    mid = rest.astype(bf16).astype(f32)
    return high, mid, rest - mid


def two_parts(value):
    high = value.astype(bf16)
    low = (value - high.astype(f32)).astype(bf16)
    return jnp.concatenate([high, low], axis=1)


def iota(shape, axis):
    return lax.broadcasted_iota(jnp.int32, shape, axis)


def put_rows(rows, shape):
    place = iota(shape, 0)
    total = jnp.zeros(shape, f32)
    for at, row in enumerate(rows):
        total = jnp.where(place == at, row, total)
    return total


def finish_kernel(img_ref, newf_ref, newl_ref, sg_ref, img_out, newf_out, newl_out, sg_out):
    img_out[...] = img_ref[...]
    newf_out[0] = newf_ref[...]
    newl_out[...] = newl_ref[...]
    for v in range(sg_ref.shape[0]):
        sg_out[v, 0] = sg_ref[v, 0:5]


def splat_kernel(
    owners, layers, views, tiles, share,
    feat_ref, logit_ref, geom_ref, dest_ref, target_ref,
    img_ref, newf_ref, newl_ref, sg_ref,
    pay, got, back, ret, pay_s, got_s, back_s, ret_s, geom8, tgt, mine_f, mine_s, gath_f, gath_s, part_f, part_s, in_f, in_s,
    img_out, img_in, perm, ids, to_slot, places, tri, tril, ones2,
    fall_s, dec_s, w_s, comp_s, keep_s, ahead_s, gk_s, res_s, run_s,
    cur_f, cur_l,
    a_send, a_recv, gf_send, gf_recv, gs_send, gs_recv,
    pf_send, pf_recv, ps_send, ps_recv, b_send, b_recv, i_send, i_recv,
    as_send, as_recv, bs_send, bs_recv, load_sem,
):
    me_t = lax.axis_index("tile")
    me_d = lax.axis_index("depth")
    owned, feats = feat_ref.shape
    cap = owned // owners
    wire = pay.dtype
    group = layers // tiles
    pixels = tiles * share
    lanes = 128
    per = lanes // cap
    my_tile = me_d // group
    partner = lax.rem(me_d + group, layers)

    def tile_peer(k):
        return lax.rem(me_t + k, owners)

    def depth_peer(k):
        return lax.rem(me_d + k, layers)

    barrier = pltpu.get_barrier_semaphore()
    for k in range(1, owners):
        pl.semaphore_signal(barrier, inc=1, device_id=(tile_peer(k), me_d), device_id_type=pl.DeviceIdType.MESH)
    for k in range(1, layers):
        pl.semaphore_signal(barrier, inc=1, device_id=(me_t, depth_peer(k)), device_id_type=pl.DeviceIdType.MESH)

    def target_copy(v, h):
        if share % lanes == 0:
            place = partner if h else me_d
            source = target_ref.at[v, my_tile, :, pl.ds(pl.multiple_of(place * share, lanes), share)]
        else:
            source = target_ref.at[v, h]
        return pltpu.make_async_copy(source, tgt.at[v, h], load_sem.at[1 + v * tiles + h])

    feature_copy = pltpu.make_async_copy(feat_ref, cur_f, load_sem.at[0])
    feature_copy.start()
    for v in range(views):
        for h in range(tiles):
            target_copy(v, h).start()
    for v in range(views):
        geom8[v] = jnp.zeros((8, owned), f32)
        geom8[v, 0:5] = geom_ref[v, 0]

    lane_row = iota((pixels, S), 0)
    pixel = lane_row + jnp.where(lane_row < share, me_d, partner - 1) * share
    places[0] = (pixel & (W - 1)).astype(f32) + 0.5
    places[1] = (pixel >> (W.bit_length() - 1)).astype(f32) + 0.5
    row = iota((S, S), 0)
    col = iota((S, S), 1)
    earlier = (row < col).astype(f32).astype(bf16)
    later_mat = (row > col).astype(f32).astype(bf16)
    ones = jnp.ones((S, S), bf16)
    half = jnp.concatenate([earlier, ones], axis=1)
    tri[...] = jnp.concatenate([half, half], axis=0)
    tril[...] = jnp.concatenate([later_mat, later_mat], axis=0)
    ones2[...] = jnp.ones((2 * feats, feats), bf16)
    cur_l[...] = logit_ref[...]

    def tile_copy(v, k, src, dst, send, recv):
        return pltpu.make_async_remote_copy(
            src_ref=src.at[v, tile_peer(k)], dst_ref=dst.at[v, me_t],
            send_sem=send.at[v, k], recv_sem=recv.at[v, k],
            device_id=(tile_peer(k), me_d), device_id_type=pl.DeviceIdType.MESH,
        )

    def exchange(v, moves, beside=None):
        for k in range(1, owners):
            for move in moves:
                tile_copy(v, k, *move).start()
        for src, dst, _, _ in moves:
            dst[v, me_t] = src[v, me_t]
        if beside is not None:
            beside()
        for k in range(1, owners):
            for move in moves:
                tile_copy(v, k, *move).wait()

    def spread(ref, v, eight):
        for t in range(owners):
            block = eight[:, (t // per) * lanes : (t // per + 1) * lanes]
            turn = (t % per) * cap
            ref[v, t] = pltpu.roll(block, lanes - turn, 1) if turn else block

    def join(ref, v):
        place = iota((8, lanes), 1) // cap
        blocks = []
        for first in range(0, owners, per):
            block = ref[v, first]
            for turn in range(1, per):
                moved = pltpu.roll(ref[v, first + turn], turn * cap, 1)
                block = jnp.where(place == turn, moved, block)
            blocks.append(block)
        return jnp.concatenate(blocks, axis=1)

    def depth_copy(v, k, src, dst, src_at, send, recv):
        return pltpu.make_async_remote_copy(
            src_ref=src.at[v, src_at], dst_ref=dst.at[v, me_d],
            send_sem=send.at[v, k], recv_sem=recv.at[v, k],
            device_id=(me_t, depth_peer(k)), device_id_type=pl.DeviceIdType.MESH,
        )

    def image_copy(v):
        return pltpu.make_async_remote_copy(
            src_ref=img_out.at[v], dst_ref=img_in.at[v],
            send_sem=i_send.at[v], recv_sem=i_recv.at[v],
            device_id=(me_t, partner), device_id_type=pl.DeviceIdType.MESH,
        )

    def slot_rows(v, e):
        g = gath_s[v, e]
        coef_a = jnp.exp(g[2:3])
        coef_c = jnp.exp(g[3:4])
        spread = jnp.exp(0.5 * (g[2:3] + g[3:4]))
        return g[0:1], g[1:2], coef_a, g[4:5] * spread, coef_c, spread, g[5:6]

    def forward(v, e):
        g0, g1, ca, cb, cc, _, opacity = slot_rows(v, e)
        dx = places[0] - g0
        dy = places[1] - g1
        quadric = ca * dx * dx + 2.0 * cb * dx * dy + cc * dy * dy
        fall = jnp.exp(-0.5 * quadric)
        coverage = jnp.minimum(opacity * fall, clamp_top)
        log_keep = jnp.log(1.0 - coverage)
        sums = dot(two_parts(log_keep), tri[...])
        decayed = jnp.exp(sums[:, :S])
        weights = (coverage * decayed).astype(bf16)
        fall_s[e] = fall
        dec_s[e] = decayed
        w_s[e] = weights
        keep_s[e] = jnp.exp(sums[:, S:])
        comp_s[e] = dot(weights, gath_f[v, e])

    def combine(v):
        res_s[...] = jnp.zeros((pixels, feats), f32)
        run_s[...] = jnp.ones((pixels, feats), f32)

        def front(e, carry):
            ahead = run_s[...]
            ahead_s[e] = ahead
            res_s[...] = res_s[...] + ahead * comp_s[e]
            run_s[...] = ahead * keep_s[e]
            return carry

        lax.fori_loop(0, layers, front, 0)
        summed = res_s[...]
        img_ref[v, my_tile] = summed[:share].T.astype(bf16)
        img_out[v] = summed[share:].T.astype(bf16)
        for h in range(tiles):
            target_copy(v, h).wait()
            res_s[h * share : (h + 1) * share] = summed[
                h * share : (h + 1) * share
            ] - tgt[v, h].astype(f32).T
        run_s[...] = jnp.zeros((pixels, feats), f32)

        def rear(i, carry):
            e = layers - 1 - i
            behind = run_s[...]
            keep = keep_s[e]
            gk_s[e] = ahead_s[e] * behind * keep
            terms = dot(two_parts(res_s[...] * comp_s[e]), ones2[...])
            run_s[...] = terms + keep * behind
            return carry

        lax.fori_loop(0, layers, rear, 0)

    def backward(v, e, out_f, out_s):
        g0, g1, ca, cb, cc, spread, opacity = slot_rows(v, e)
        grad_comp = (ahead_s[e] * res_s[...]).astype(bf16)
        out_f[v, e] = dot(w_s[e], grad_comp, 0, 0).astype(bf16)
        grad_weight = dot(grad_comp, gath_f[v, e], 1, 1)
        decayed = dec_s[e]
        fall = fall_s[e]
        product = opacity * fall
        coverage = jnp.minimum(product, clamp_top)
        grad_decayed = grad_weight * decayed
        later = dot(two_parts(grad_decayed * coverage), tril[...])
        grad_log = later + gk_s[e]
        grad_coverage = grad_decayed - grad_log / (1.0 - coverage)
        moment = fall * jnp.where(product < clamp_top, grad_coverage, 0.0)
        dx = places[0] - g0
        dy = places[1] - g1
        moment_x = moment * dx
        moment_y = moment * dy

        def total(value):
            return jnp.sum(value, axis=0, keepdims=True)

        m0 = total(moment)
        mx = opacity * total(moment_x)
        my = opacity * total(moment_y)
        first = -0.5 * opacity * total(moment_x * dx)
        cross = -1.0 * opacity * total(moment_x * dy)
        second = -0.5 * opacity * total(moment_y * dy)
        out_s[v, e] = put_rows(
            [
                ca * mx + cb * my,
                cb * mx + cc * my,
                ca * first + 0.5 * cb * cross,
                cc * second + 0.5 * cb * cross,
                spread * cross,
                opacity * (1.0 - opacity) * m0,
            ],
            (8, S),
        )

    def move_rows(eight, onehot, side):
        high, mid, low = three_parts(eight)
        rows = jnp.concatenate([high, mid, low, jnp.zeros_like(low)], axis=0)
        moved = dot(rows.astype(bf16), onehot, 1, side)
        return moved[0:8] + moved[8:16] + moved[16:24]

    def pack(ref, v, value):
        ref[v] = value.reshape(owners, cap, feats).astype(wire)

    def unpack(ref, v):
        return ref[v].astype(f32).reshape(owned, feats).astype(bf16)

    def indices(v):
        dest = dest_ref[v]
        low_edge = iota((owners, owned), 0) * owned
        hit = (dest >= low_edge) & (dest < low_edge + owned)
        matches = hit.astype(f32)
        upper = (iota((owned, owned), 0) < iota((owned, owned), 1)).astype(f32).astype(bf16)
        rank = dot(matches.astype(bf16), upper)
        count = iota((owners, owned), 0).astype(f32) * cap + rank + 1.0
        position = jnp.sum(matches * count, axis=0, keepdims=True) - 1.0
        ids[v] = jnp.sum(
            matches * (dest - low_edge + 1).astype(f32), axis=0, keepdims=True
        )
        perm[v] = (iota((owned, owned), 0).astype(f32) == position).astype(f32).astype(bf16)

    def dispatch(v):
        opacity = 1.0 / (1.0 + jnp.exp(-cur_l[...]))
        rows8 = iota((8, owned), 0)
        eight = jnp.where(rows8 == 5, opacity, jnp.where(rows8 == 6, ids[v], geom8[v]))
        pack(pay, v, dot(perm[v], cur_f[...]))
        spread(pay_s, v, move_rows(eight, perm[v], 1))

    def later_indices():
        for v in range(1, views):
            indices(v)

    indices(0)
    feature_copy.wait()
    for v in range(views):
        dispatch(v)
        if v == 0:
            pl.semaphore_wait(barrier, owners + layers - 2)
        exchange(
            v,
            [(pay_s, got_s, as_send, as_recv), (pay, got, a_send, a_recv)],
            later_indices if v == 0 else None,
        )
        arrived = join(got_s, v)
        slots = (iota((owned, owned), 0).astype(f32) + 1.0 == arrived[6:7, :]).astype(f32).astype(bf16)
        to_slot[v] = slots
        slot_f = dot(slots, unpack(got, v)).astype(bf16)
        shapes = move_rows(arrived, slots, 1)
        for t in range(tiles):
            mine_f[v, t] = slot_f[t * S : (t + 1) * S]
            mine_s[v, t] = shapes[:, t * S : (t + 1) * S]

        def gather(k):
            there = depth_peer(k) // group
            return (
                depth_copy(v, k, mine_f, gath_f, there, gf_send, gf_recv),
                depth_copy(v, k, mine_s, gath_s, there, gs_send, gs_recv),
            )

        for k in range(1, layers):
            for copy in gather(k):
                copy.start()
        gath_f[v, me_d] = mine_f[v, my_tile]
        gath_s[v, me_d] = mine_s[v, my_tile]
        forward(v, me_d)

        def fwd_step(k, carry):
            for copy in gather(k):
                copy.wait()
            forward(v, lax.rem(me_d + layers - k, layers))
            return carry

        lax.fori_loop(1, layers, fwd_step, 0)
        combine(v)

        def give(k):
            e = depth_peer(k)
            return (
                depth_copy(v, k, part_f, in_f, e, pf_send, pf_recv),
                depth_copy(v, k, part_s, in_s, e, ps_send, ps_recv),
            )

        def bwd_step(k, carry):
            backward(v, depth_peer(k), part_f, part_s)
            for copy in give(k):
                copy.start()
            return carry

        lax.fori_loop(1, layers, bwd_step, 0)
        backward(v, me_d, in_f, in_s)
        for k in range(1, layers):
            for copy in give(k):
                copy.wait()
        image_copy(v).start()
        sums_f = []
        sums_s = []
        for t in range(tiles):
            sums_f.append(sum(in_f[v, z].astype(f32) for z in range(t * group, (t + 1) * group)))
            sums_s.append(sum(in_s[v, z] for z in range(t * group, (t + 1) * group)))
        sum_f = jnp.concatenate(sums_f, axis=0)
        sum_s = jnp.concatenate(sums_s, axis=1)
        pack(back, v, dot(to_slot[v], sum_f.astype(bf16), 0, 0))
        spread(back_s, v, move_rows(sum_s, to_slot[v], 0))
        exchange(v, [(back, ret, b_send, b_recv), (back_s, ret_s, bs_send, bs_recv)])
        grad_feat = dot(perm[v], unpack(ret, v), 0, 0)
        grad_eight = move_rows(join(ret_s, v), perm[v], 0)
        sg_ref[v] = grad_eight
        cur_f[...] = (cur_f[...].astype(f32) - feature_rate * grad_feat).astype(bf16)
        cur_l[...] = cur_l[...] - opacity_rate * grad_eight[5:6]

    for v in range(views):
        image_copy(v).wait()
        img_ref[v, 1 - my_tile] = img_in[v]
    newf_ref[...] = cur_f[...]
    newl_ref[...] = cur_l[...]


def body(features, logits, geometry, dest_slot, target):
    owners = lax.axis_size("tile")
    layers = lax.axis_size("depth")
    depth_here = lax.axis_index("depth")
    views, tiles, feats, pixels = target.shape
    owned = features.shape[1]
    cap = owned // owners
    share = pixels // layers
    wire = bf16 if cap % 16 == 0 else f32
    if tiles != 2 or layers % tiles or 128 % cap:
        raise ValueError("unsupported split")
    if share % 128:
        group = layers // tiles
        tile_here = depth_here // group
        partner = lax.rem(depth_here + group, layers)
        target = jnp.concatenate(
            [
                lax.dynamic_slice(
                    target, (0, tile_here, 0, place * share), (views, 1, feats, share)
                )
                for place in (depth_here, partner)
            ],
            axis=1,
        )
    hbm = pl.BlockSpec(memory_space=pl.ANY)
    vm = pl.BlockSpec(memory_space=pltpu.VMEM)
    grid = (layers, tiles * share, S)
    dma = pltpu.SemaphoreType.DMA
    images, new_f, new_l, grads = pl.pallas_call(
        functools.partial(splat_kernel, owners, layers, views, tiles, share),
        out_shape=(
            jax.ShapeDtypeStruct((views, tiles, feats, share), bf16),
            jax.ShapeDtypeStruct((owned, feats), bf16),
            jax.ShapeDtypeStruct((1, owned), f32),
            jax.ShapeDtypeStruct((views, 8, owned), f32),
        ),
        in_specs=[hbm, vm, vm, vm, hbm],
        out_specs=(vm,) * 4,
        scratch_shapes=[
            pltpu.VMEM((views, owners, cap, feats), wire),
            pltpu.VMEM((views, owners, cap, feats), wire),
            pltpu.VMEM((views, owners, cap, feats), wire),
            pltpu.VMEM((views, owners, cap, feats), wire),
            pltpu.VMEM((views, owners, 8, 128), f32),
            pltpu.VMEM((views, owners, 8, 128), f32),
            pltpu.VMEM((views, owners, 8, 128), f32),
            pltpu.VMEM((views, owners, 8, 128), f32),
            pltpu.VMEM((views, 8, owned), f32),
            pltpu.VMEM((views, tiles, feats, share), bf16),
            pltpu.VMEM((views, tiles, S, feats), bf16),
            pltpu.VMEM((views, tiles, 8, S), f32),
            pltpu.VMEM((views, layers, S, feats), bf16),
            pltpu.VMEM((views, layers, 8, S), f32),
            pltpu.VMEM((views, layers, S, feats), bf16),
            pltpu.VMEM((views, layers, 8, S), f32),
            pltpu.VMEM((views, layers, S, feats), bf16),
            pltpu.VMEM((views, layers, 8, S), f32),
            pltpu.VMEM((views, feats, share), bf16),
            pltpu.VMEM((views, feats, share), bf16),
            pltpu.VMEM((views, owned, owned), bf16),
            pltpu.VMEM((views, 1, owned), f32),
            pltpu.VMEM((views, owned, owned), bf16),
            pltpu.VMEM((2, tiles * share, S), f32),
            pltpu.VMEM((2 * S, 2 * S), bf16),
            pltpu.VMEM((2 * S, S), bf16),
            pltpu.VMEM((2 * feats, feats), bf16),
            pltpu.VMEM(grid, f32),
            pltpu.VMEM(grid, f32),
            pltpu.VMEM(grid, bf16),
            pltpu.VMEM(grid, f32),
            pltpu.VMEM(grid, f32),
            pltpu.VMEM(grid, f32),
            pltpu.VMEM(grid, f32),
            pltpu.VMEM((tiles * share, feats), f32),
            pltpu.VMEM((tiles * share, feats), f32),
            pltpu.VMEM((owned, feats), bf16),
            pltpu.VMEM((1, owned), f32),
            dma((views, owners)), dma((views, owners)),
            dma((views, layers)), dma((views, layers)),
            dma((views, layers)), dma((views, layers)),
            dma((views, layers)), dma((views, layers)),
            dma((views, layers)), dma((views, layers)),
            dma((views, owners)), dma((views, owners)),
            dma((views,)), dma((views,)),
            dma((views, owners)), dma((views, owners)),
            dma((views, owners)), dma((views, owners)),
            dma((1 + views * tiles,)),
        ],
        compiler_params=pltpu.CompilerParams(
            collective_id=0, has_side_effects=True, vmem_limit_bytes=56 * 1024 * 1024
        ),
        name="splat_views",
    )(features[0], logits, geometry, dest_slot, target)
    return pl.pallas_call(
        finish_kernel,
        out_shape=(
            jax.ShapeDtypeStruct(images.shape, bf16),
            jax.ShapeDtypeStruct((1, owned, feats), bf16),
            jax.ShapeDtypeStruct((1, owned), f32),
            jax.ShapeDtypeStruct((views, 1, 5, owned), f32),
        ),
        in_specs=[vm] * 4,
        out_specs=(vm,) * 4,
        name="write_outputs",
    )(images, new_f, new_l, grads)


def solution(mesh):
    placed = (
        P("depth", "tile", None),
        P("depth", "tile"),
        P(None, "depth", None, "tile"),
        P(None, "depth", "tile"),
        P(None, "tile", None, None),
    )
    return jax.shard_map(
        body,
        mesh=mesh,
        in_specs=placed,
        out_specs=(
            P(None, "tile", None, "depth"),
            P("depth", "tile", None),
            P("depth", "tile"),
            P(None, "depth", None, "tile"),
        ),
        check_vma=False,
    )
```

```python
import functools

import jax
import jax.numpy as jnp
from jax import lax
from jax.experimental import pallas as pl
from jax.experimental.pallas import tpu as pltpu
from jax.sharding import PartitionSpec as P

W = 32
S = 128
clamp_top = 0.99
feature_rate = 0.5
opacity_rate = 0.5
f32 = jnp.float32
bf16 = jnp.bfloat16


def dot(lhs, rhs, left=1, right=0):
    return lax.dot_general(
        lhs, rhs, (((left,), (right,)), ((), ())), preferred_element_type=f32
    )


def three_parts(value):
    high = value.astype(bf16).astype(f32)
    rest = value - high
    mid = rest.astype(bf16).astype(f32)
    return high, mid, rest - mid


def two_parts(value):
    high = value.astype(bf16)
    low = (value - high.astype(f32)).astype(bf16)
    return jnp.concatenate([high, low], axis=1)


def iota(shape, axis):
    return lax.broadcasted_iota(jnp.int32, shape, axis)


def put_rows(rows, shape):
    place = iota(shape, 0)
    total = jnp.zeros(shape, f32)
    for at, row in enumerate(rows):
        total = jnp.where(place == at, row, total)
    return total


def finish_kernel(img_ref, newf_ref, newl_ref, sg_ref, img_out, newf_out, newl_out, sg_out):
    img_out[...] = img_ref[...]
    newf_out[0] = newf_ref[...]
    newl_out[...] = newl_ref[...]
    for v in range(sg_ref.shape[0]):
        for r in range(5):
            sg_out[v, r] = sg_ref[v, r : r + 1]


def paired(me, k, count):
    place, total = 1, 0
    while place < count:
        total = total + place * lax.rem(lax.div(me, place) + lax.rem(lax.div(k, place), 2), 2)
        place *= 2
    return total


def steps(first, last, body):
    if last - first <= 4:
        for at in range(first, last):
            body(at)
    else:
        lax.fori_loop(first, last, lambda at, carry: (body(at), carry)[1], 0)


def splat_kernel(
    owners, layers, views, tiles, share,
    feat_ref, logit_ref, geom_ref, dest_ref, target_ref,
    img_ref, newf_ref, newl_ref, sg_ref,
    pay, got, back, ret, pay_s, got_s, back_s, ret_s, geom8, tgt, mine_f, mine_s, gath_f, gath_s, part_f, part_s, in_f, in_s,
    img_out, img_in, perm, ids, to_slot, places, tri, tril, ones2,
    fall_s, dec_s, w_s, comp_s, keep_s, ahead_s, gk_s, res_s, run_s,
    cur_f, cur_l,
    a_send, a_recv, gf_send, gf_recv, gs_send, gs_recv,
    pf_send, pf_recv, ps_send, ps_recv, b_send, b_recv, i_send, i_recv,
    as_send, as_recv, bs_send, bs_recv, load_sem,
):
    me_t = lax.axis_index("tile")
    me_d = lax.axis_index("depth")
    owned, feats = feat_ref.shape
    cap = owned // owners
    wire = pay.dtype
    group = layers // tiles
    pixels = tiles * share
    lanes = 128
    per = lanes // cap
    my_tile = me_d // group
    partner = lax.rem(me_d + group, layers)

    def tile_peer(k):
        return paired(me_t, k, owners)

    def depth_peer(k):
        return paired(me_d, k, layers)

    barrier = pltpu.get_barrier_semaphore()
    for k in range(1, owners):
        pl.semaphore_signal(barrier, inc=1, device_id=(tile_peer(k), me_d), device_id_type=pl.DeviceIdType.MESH)
    for k in range(1, layers):
        pl.semaphore_signal(barrier, inc=1, device_id=(me_t, depth_peer(k)), device_id_type=pl.DeviceIdType.MESH)

    def target_copy(v, h):
        if share % lanes == 0:
            place = partner if h else me_d
            source = target_ref.at[v, my_tile, :, pl.ds(pl.multiple_of(place * share, lanes), share)]
        else:
            source = target_ref.at[v, h]
        return pltpu.make_async_copy(source, tgt.at[v, h], load_sem.at[1 + v * tiles + h])

    feature_copy = pltpu.make_async_copy(feat_ref, cur_f, load_sem.at[0])
    feature_copy.start()
    for v in range(views):
        for h in range(tiles):
            target_copy(v, h).start()
    for v in range(views):
        geom8[v] = jnp.zeros((8, owned), f32)
        for r in range(5):
            geom8[v, r : r + 1] = geom_ref[v, r]

    lane_row = iota((pixels, S), 0)
    pixel = lane_row + jnp.where(lane_row < share, me_d, partner - 1) * share
    places[0] = (pixel & (W - 1)).astype(f32) + 0.5
    places[1] = (pixel >> (W.bit_length() - 1)).astype(f32) + 0.5
    row = iota((S, S), 0)
    col = iota((S, S), 1)
    earlier = (row < col).astype(f32).astype(bf16)
    later_mat = (row > col).astype(f32).astype(bf16)
    ones = jnp.ones((S, S), bf16)
    half = jnp.concatenate([earlier, ones], axis=1)
    tri[...] = jnp.concatenate([half, half], axis=0)
    tril[...] = jnp.concatenate([later_mat, later_mat], axis=0)
    ones2[...] = jnp.ones((2 * feats, feats), bf16)
    cur_l[...] = logit_ref[...]

    def tile_copy(v, k, src, dst, send, recv):
        return pltpu.make_async_remote_copy(
            src_ref=src.at[v, tile_peer(k)], dst_ref=dst.at[v, me_t],
            send_sem=send.at[v, k], recv_sem=recv.at[v, k],
            device_id=(tile_peer(k), me_d), device_id_type=pl.DeviceIdType.MESH,
        )

    def exchange(v, moves, beside=None):
        for k in range(owners - 1, 0, -1):
            for move in moves:
                tile_copy(v, k, *move).start()
        for src, dst, _, _ in moves:
            dst[v, me_t] = src[v, me_t]
        if beside is not None:
            beside()
        for k in range(1, owners):
            for move in moves:
                tile_copy(v, k, *move).wait()

    def spread(ref, v, eight):
        for t in range(owners):
            block = eight[:, (t // per) * lanes : (t // per + 1) * lanes]
            turn = (t % per) * cap
            ref[v, t] = pltpu.roll(block, lanes - turn, 1) if turn else block

    def join(ref, v):
        place = iota((8, lanes), 1) // cap
        blocks = []
        for first in range(0, owners, per):
            block = ref[v, first]
            for turn in range(1, per):
                moved = pltpu.roll(ref[v, first + turn], turn * cap, 1)
                block = jnp.where(place == turn, moved, block)
            blocks.append(block)
        return jnp.concatenate(blocks, axis=1)

    def depth_copy(v, k, src, dst, src_at, send, recv):
        return pltpu.make_async_remote_copy(
            src_ref=src.at[v, src_at], dst_ref=dst.at[v, me_d],
            send_sem=send.at[v, k], recv_sem=recv.at[v, k],
            device_id=(me_t, depth_peer(k)), device_id_type=pl.DeviceIdType.MESH,
        )

    def image_copy(v):
        return pltpu.make_async_remote_copy(
            src_ref=img_out.at[v], dst_ref=img_in.at[v],
            send_sem=i_send.at[v], recv_sem=i_recv.at[v],
            device_id=(me_t, partner), device_id_type=pl.DeviceIdType.MESH,
        )

    def slot_rows(v, e):
        g = gath_s[v, e]
        coef_a = jnp.exp(g[2:3])
        coef_c = jnp.exp(g[3:4])
        spread = jnp.exp(0.5 * (g[2:3] + g[3:4]))
        return g[0:1], g[1:2], coef_a, g[4:5] * spread, coef_c, spread, g[5:6]

    def forward(v, e):
        g0, g1, ca, cb, cc, _, opacity = slot_rows(v, e)
        dx = places[0] - g0
        dy = places[1] - g1
        quadric = ca * dx * dx + 2.0 * cb * dx * dy + cc * dy * dy
        fall = jnp.exp(-0.5 * quadric)
        coverage = jnp.minimum(opacity * fall, clamp_top)
        log_keep = jnp.log(1.0 - coverage)
        sums = dot(two_parts(log_keep), tri[...])
        decayed = jnp.exp(sums[:, :S])
        weights = (coverage * decayed).astype(bf16)
        fall_s[e] = fall
        dec_s[e] = decayed
        w_s[e] = weights
        keep_s[e] = jnp.exp(sums[:, S:])
        comp_s[e] = dot(weights, gath_f[v, e])

    def combine(v):
        res_s[...] = jnp.zeros((pixels, feats), f32)
        run_s[...] = jnp.ones((pixels, feats), f32)

        def front(e):
            ahead = run_s[...]
            ahead_s[e] = ahead
            res_s[...] = res_s[...] + ahead * comp_s[e]
            run_s[...] = ahead * keep_s[e]

        steps(0, layers, front)
        summed = res_s[...]
        img_ref[v, my_tile] = summed[:share].T.astype(bf16)
        img_out[v] = summed[share:].T.astype(bf16)
        for h in range(tiles):
            target_copy(v, h).wait()
            res_s[h * share : (h + 1) * share] = summed[
                h * share : (h + 1) * share
            ] - tgt[v, h].astype(f32).T
        run_s[...] = jnp.zeros((pixels, feats), f32)

        def rear(i):
            e = layers - 1 - i
            behind = run_s[...]
            keep = keep_s[e]
            gk_s[e] = ahead_s[e] * behind * keep
            terms = dot(two_parts(res_s[...] * comp_s[e]), ones2[...])
            run_s[...] = terms + keep * behind

        steps(0, layers - 1, rear)
        gk_s[0] = ahead_s[0] * run_s[...] * keep_s[0]

    def backward(v, e, out_f, out_s):
        g0, g1, ca, cb, cc, spread, opacity = slot_rows(v, e)
        grad_comp = (ahead_s[e] * res_s[...]).astype(bf16)
        out_f[v, e] = dot(w_s[e], grad_comp, 0, 0).astype(bf16)
        grad_weight = dot(grad_comp, gath_f[v, e], 1, 1)
        decayed = dec_s[e]
        fall = fall_s[e]
        product = opacity * fall
        coverage = jnp.minimum(product, clamp_top)
        grad_decayed = grad_weight * decayed
        later = dot(two_parts(grad_decayed * coverage), tril[...])
        grad_log = later + gk_s[e]
        grad_coverage = grad_decayed - grad_log / (1.0 - coverage)
        moment = fall * jnp.where(product < clamp_top, grad_coverage, 0.0)
        dx = places[0] - g0
        dy = places[1] - g1
        moment_x = moment * dx
        moment_y = moment * dy

        def total(value):
            return jnp.sum(value, axis=0, keepdims=True)

        m0 = total(moment)
        mx = opacity * total(moment_x)
        my = opacity * total(moment_y)
        first = -0.5 * opacity * total(moment_x * dx)
        cross = -1.0 * opacity * total(moment_x * dy)
        second = -0.5 * opacity * total(moment_y * dy)
        out_s[v, e] = put_rows(
            [
                ca * mx + cb * my,
                cb * mx + cc * my,
                ca * first + 0.5 * cb * cross,
                cc * second + 0.5 * cb * cross,
                spread * cross,
                opacity * (1.0 - opacity) * m0,
            ],
            (8, S),
        )

    def move_rows(eight, onehot, side):
        high, mid, low = three_parts(eight)
        rows = jnp.concatenate([high, mid, low, jnp.zeros_like(low)], axis=0)
        moved = dot(rows.astype(bf16), onehot, 1, side)
        return moved[0:8] + moved[8:16] + moved[16:24]

    def pack(ref, v, value):
        ref[v] = value.reshape(owners, cap, feats).astype(wire)

    def unpack(ref, v):
        return ref[v].astype(f32).reshape(owned, feats).astype(bf16)

    def indices(v):
        dest = dest_ref[v]
        low_edge = iota((owners, owned), 0) * owned
        hit = (dest >= low_edge) & (dest < low_edge + owned)
        matches = hit.astype(f32)
        upper = (iota((owned, owned), 0) < iota((owned, owned), 1)).astype(f32).astype(bf16)
        rank = dot(matches.astype(bf16), upper)
        count = iota((owners, owned), 0).astype(f32) * cap + rank + 1.0
        position = jnp.sum(matches * count, axis=0, keepdims=True) - 1.0
        ids[v] = jnp.sum(
            matches * (dest - low_edge + 1).astype(f32), axis=0, keepdims=True
        )
        perm[v] = (iota((owned, owned), 0).astype(f32) == position).astype(f32).astype(bf16)

    def dispatch(v):
        opacity = 1.0 / (1.0 + jnp.exp(-cur_l[...]))
        rows8 = iota((8, owned), 0)
        eight = jnp.where(rows8 == 5, opacity, jnp.where(rows8 == 6, ids[v], geom8[v]))
        pack(pay, v, dot(perm[v], cur_f[...]))
        spread(pay_s, v, move_rows(eight, perm[v], 1))

    def later_indices():
        for v in range(1, views):
            indices(v)

    indices(0)
    feature_copy.wait()
    for v in range(views):
        dispatch(v)
        if v == 0:
            pl.semaphore_wait(barrier, owners + layers - 2)
        exchange(
            v,
            [(pay_s, got_s, as_send, as_recv), (pay, got, a_send, a_recv)],
            later_indices if v == 0 else None,
        )
        arrived = join(got_s, v)
        slots = (iota((owned, owned), 0).astype(f32) + 1.0 == arrived[6:7, :]).astype(f32).astype(bf16)
        to_slot[v] = slots
        slot_f = dot(slots, unpack(got, v)).astype(bf16)
        shapes = move_rows(arrived, slots, 1)
        for t in range(tiles):
            mine_f[v, t] = slot_f[t * S : (t + 1) * S]
            mine_s[v, t] = shapes[:, t * S : (t + 1) * S]

        def gather(k):
            there = depth_peer(k) // group
            return (
                depth_copy(v, k, mine_f, gath_f, there, gf_send, gf_recv),
                depth_copy(v, k, mine_s, gath_s, there, gs_send, gs_recv),
            )

        for k in range(layers - 1, 0, -1):
            for copy in gather(k):
                copy.start()
        gath_f[v, me_d] = mine_f[v, my_tile]
        gath_s[v, me_d] = mine_s[v, my_tile]
        forward(v, me_d)

        def fwd_step(i):
            k = layers - i
            for copy in gather(k):
                copy.wait()
            forward(v, depth_peer(k))

        steps(1, layers, fwd_step)
        combine(v)

        def give(k):
            e = depth_peer(k)
            return (
                depth_copy(v, k, part_f, in_f, e, pf_send, pf_recv),
                depth_copy(v, k, part_s, in_s, e, ps_send, ps_recv),
            )

        def bwd_step(i):
            k = layers - i
            backward(v, depth_peer(k), part_f, part_s)
            for copy in give(k):
                copy.start()

        steps(1, layers, bwd_step)
        backward(v, me_d, in_f, in_s)
        for k in range(1, layers):
            for copy in give(k):
                copy.wait()
        image_copy(v).start()
        sums_f = []
        sums_s = []
        for t in range(tiles):
            sums_f.append(sum(in_f[v, z].astype(f32) for z in range(t * group, (t + 1) * group)))
            sums_s.append(sum(in_s[v, z] for z in range(t * group, (t + 1) * group)))
        sum_f = jnp.concatenate(sums_f, axis=0)
        sum_s = jnp.concatenate(sums_s, axis=1)
        pack(back, v, dot(to_slot[v], sum_f.astype(bf16), 0, 0))
        spread(back_s, v, move_rows(sum_s, to_slot[v], 0))
        exchange(v, [(back, ret, b_send, b_recv), (back_s, ret_s, bs_send, bs_recv)])
        grad_feat = dot(perm[v], unpack(ret, v), 0, 0)
        grad_eight = move_rows(join(ret_s, v), perm[v], 0)
        sg_ref[v] = grad_eight
        cur_f[...] = (cur_f[...].astype(f32) - feature_rate * grad_feat).astype(bf16)
        cur_l[...] = cur_l[...] - opacity_rate * grad_eight[5:6]

    for v in range(views):
        image_copy(v).wait()
        img_ref[v, 1 - my_tile] = img_in[v]
    newf_ref[...] = cur_f[...]
    newl_ref[...] = cur_l[...]


def body(features, logits, geometry, dest_slot, target):
    owners = lax.axis_size("tile")
    layers = lax.axis_size("depth")
    depth_here = lax.axis_index("depth")
    views, tiles, feats, pixels = target.shape
    owned = features.shape[1]
    cap = owned // owners
    share = pixels // layers
    wire = bf16 if cap % 16 == 0 else f32
    if tiles != 2 or layers % tiles or 128 % cap or layers & (layers - 1) or owners & (owners - 1):
        raise ValueError("unsupported split")
    if share % 128:
        group = layers // tiles
        tile_here = depth_here // group
        partner = lax.rem(depth_here + group, layers)
        target = jnp.concatenate(
            [
                lax.dynamic_slice(
                    target, (0, tile_here, 0, place * share), (views, 1, feats, share)
                )
                for place in (depth_here, partner)
            ],
            axis=1,
        )
    hbm = pl.BlockSpec(memory_space=pl.ANY)
    vm = pl.BlockSpec(memory_space=pltpu.VMEM)
    grid = (layers, tiles * share, S)
    dma = pltpu.SemaphoreType.DMA
    images, new_f, new_l, grads = pl.pallas_call(
        functools.partial(splat_kernel, owners, layers, views, tiles, share),
        out_shape=(
            jax.ShapeDtypeStruct((views, tiles, feats, share), bf16),
            jax.ShapeDtypeStruct((owned, feats), bf16),
            jax.ShapeDtypeStruct((1, owned), f32),
            jax.ShapeDtypeStruct((views, 8, owned), f32),
        ),
        in_specs=[hbm, vm, vm, vm, hbm],
        out_specs=(vm,) * 4,
        scratch_shapes=[
            pltpu.VMEM((views, owners, cap, feats), wire),
            pltpu.VMEM((views, owners, cap, feats), wire),
            pltpu.VMEM((views, owners, cap, feats), wire),
            pltpu.VMEM((views, owners, cap, feats), wire),
            pltpu.VMEM((views, owners, 8, 128), f32),
            pltpu.VMEM((views, owners, 8, 128), f32),
            pltpu.VMEM((views, owners, 8, 128), f32),
            pltpu.VMEM((views, owners, 8, 128), f32),
            pltpu.VMEM((views, 8, owned), f32),
            pltpu.VMEM((views, tiles, feats, share), bf16),
            pltpu.VMEM((views, tiles, S, feats), bf16),
            pltpu.VMEM((views, tiles, 8, S), f32),
            pltpu.VMEM((views, layers, S, feats), bf16),
            pltpu.VMEM((views, layers, 8, S), f32),
            pltpu.VMEM((views, layers, S, feats), bf16),
            pltpu.VMEM((views, layers, 8, S), f32),
            pltpu.VMEM((views, layers, S, feats), bf16),
            pltpu.VMEM((views, layers, 8, S), f32),
            pltpu.VMEM((views, feats, share), bf16),
            pltpu.VMEM((views, feats, share), bf16),
            pltpu.VMEM((views, owned, owned), bf16),
            pltpu.VMEM((views, 1, owned), f32),
            pltpu.VMEM((views, owned, owned), bf16),
            pltpu.VMEM((2, tiles * share, S), f32),
            pltpu.VMEM((2 * S, 2 * S), bf16),
            pltpu.VMEM((2 * S, S), bf16),
            pltpu.VMEM((2 * feats, feats), bf16),
            pltpu.VMEM(grid, f32),
            pltpu.VMEM(grid, f32),
            pltpu.VMEM(grid, bf16),
            pltpu.VMEM(grid, f32),
            pltpu.VMEM(grid, f32),
            pltpu.VMEM(grid, f32),
            pltpu.VMEM(grid, f32),
            pltpu.VMEM((tiles * share, feats), f32),
            pltpu.VMEM((tiles * share, feats), f32),
            pltpu.VMEM((owned, feats), bf16),
            pltpu.VMEM((1, owned), f32),
            dma((views, owners)), dma((views, owners)),
            dma((views, layers)), dma((views, layers)),
            dma((views, layers)), dma((views, layers)),
            dma((views, layers)), dma((views, layers)),
            dma((views, layers)), dma((views, layers)),
            dma((views, owners)), dma((views, owners)),
            dma((views,)), dma((views,)),
            dma((views, owners)), dma((views, owners)),
            dma((views, owners)), dma((views, owners)),
            dma((1 + views * tiles,)),
        ],
        compiler_params=pltpu.CompilerParams(
            collective_id=0, has_side_effects=True, vmem_limit_bytes=56 * 1024 * 1024
        ),
        name="splat_views",
    )(features[0], logits, geometry.transpose(0, 2, 1, 3), dest_slot, target)
    images, new_f, new_l, grads = pl.pallas_call(
        finish_kernel,
        out_shape=(
            jax.ShapeDtypeStruct(images.shape, bf16),
            jax.ShapeDtypeStruct((1, owned, feats), bf16),
            jax.ShapeDtypeStruct((1, owned), f32),
            jax.ShapeDtypeStruct((views, 5, 1, owned), f32),
        ),
        in_specs=[vm] * 4,
        out_specs=(vm,) * 4,
        name="write_outputs",
    )(images, new_f, new_l, grads)
    return images, new_f, new_l, grads.transpose(0, 2, 1, 3)


def solution(mesh):
    placed = (
        P("depth", "tile", None),
        P("depth", "tile"),
        P(None, "depth", None, "tile"),
        P(None, "depth", "tile"),
        P(None, "tile", None, None),
    )
    return jax.shard_map(
        body,
        mesh=mesh,
        in_specs=placed,
        out_specs=(
            P(None, "tile", None, "depth"),
            P("depth", "tile", None),
            P("depth", "tile"),
            P(None, "depth", None, "tile"),
        ),
        check_vma=False,
    )
```

```python
import functools

import jax
import jax.numpy as jnp
from jax import lax
from jax.experimental import pallas as pl
from jax.experimental.pallas import tpu as pltpu
from jax.sharding import PartitionSpec as P

W = 32
S = 128
clamp_top = 0.99
feature_rate = 0.5
opacity_rate = 0.5
f32 = jnp.float32
bf16 = jnp.bfloat16


def dot(lhs, rhs, left=1, right=0):
    return lax.dot_general(
        lhs, rhs, (((left,), (right,)), ((), ())), preferred_element_type=f32
    )


def three_parts(value):
    high = value.astype(bf16).astype(f32)
    rest = value - high
    mid = rest.astype(bf16).astype(f32)
    return high, mid, rest - mid


def two_parts(value):
    high = value.astype(bf16)
    low = (value - high.astype(f32)).astype(bf16)
    return jnp.concatenate([high, low], axis=1)


def iota(shape, axis):
    return lax.broadcasted_iota(jnp.int32, shape, axis)


def put_rows(rows, shape):
    place = iota(shape, 0)
    total = jnp.zeros(shape, f32)
    for at, row in enumerate(rows):
        total = jnp.where(place == at, row, total)
    return total


def finish_kernel(img_ref, newf_ref, newl_ref, sg_ref, img_out, newf_out, newl_out, sg_out):
    img_out[...] = img_ref[...]
    newf_out[0] = newf_ref[...]
    newl_out[...] = newl_ref[...]
    for v in range(sg_ref.shape[0]):
        for r in range(5):
            sg_out[v, r] = sg_ref[v, r : r + 1]


def paired(me, k, count):
    place, total = 1, 0
    while place < count:
        total = total + place * lax.rem(lax.div(me, place) + lax.rem(lax.div(k, place), 2), 2)
        place *= 2
    return total


def steps(first, last, body):
    if last - first <= 4:
        for at in range(first, last):
            body(at)
    else:
        lax.fori_loop(first, last, lambda at, carry: (body(at), carry)[1], 0)


def splat_kernel(
    owners, layers, views, tiles, share,
    feat_ref, logit_ref, geom_ref, dest_ref, target_ref,
    img_ref, newf_ref, newl_ref, sg_ref,
    pay, got, back, ret, pay_s, got_s, back_s, ret_s, geom8, tgt, mine_f, mine_s, gath_f, gath_s, part_f, part_s, in_f, in_s,
    img_out, img_in, perm, ids, to_slot, places, tri, tril, ones2,
    fall_s, dec_s, w_s, comp_s, keep_s, ahead_s, gk_s, res_s, run_s,
    cur_f, cur_l,
    a_send, a_recv, gf_send, gf_recv, gs_send, gs_recv,
    pf_send, pf_recv, ps_send, ps_recv, b_send, b_recv, i_send, i_recv,
    as_send, as_recv, bs_send, bs_recv, load_sem,
):
    me_t = lax.axis_index("tile")
    me_d = lax.axis_index("depth")
    owned, feats = feat_ref.shape
    cap = owned // owners
    wire = pay.dtype
    group = layers // tiles
    pixels = tiles * share
    lanes = 128
    per = lanes // cap
    my_tile = me_d // group
    partner = lax.rem(me_d + group, layers)

    def tile_peer(k):
        return paired(me_t, k, owners)

    def depth_peer(k):
        return paired(me_d, k, layers)

    barrier = pltpu.get_barrier_semaphore()
    for k in range(1, owners):
        pl.semaphore_signal(barrier, inc=1, device_id=(tile_peer(k), me_d), device_id_type=pl.DeviceIdType.MESH)
    for k in range(1, layers):
        pl.semaphore_signal(barrier, inc=1, device_id=(me_t, depth_peer(k)), device_id_type=pl.DeviceIdType.MESH)

    def target_copy(v, h):
        if share % lanes == 0:
            place = partner if h else me_d
            source = target_ref.at[v, my_tile, :, pl.ds(pl.multiple_of(place * share, lanes), share)]
        else:
            source = target_ref.at[v, h]
        return pltpu.make_async_copy(source, tgt.at[v, h], load_sem.at[1 + v * tiles + h])

    feature_copy = pltpu.make_async_copy(feat_ref, cur_f, load_sem.at[0])
    feature_copy.start()
    for v in range(views):
        for h in range(tiles):
            target_copy(v, h).start()
    for v in range(views):
        geom8[v] = jnp.zeros((8, owned), f32)
        for r in range(5):
            geom8[v, r : r + 1] = geom_ref[v, r]

    lane_row = iota((pixels, S), 0)
    pixel = lane_row + jnp.where(lane_row < share, me_d, partner - 1) * share
    places[0] = (pixel & (W - 1)).astype(f32) + 0.5
    places[1] = (pixel >> (W.bit_length() - 1)).astype(f32) + 0.5
    row = iota((S, S), 0)
    col = iota((S, S), 1)
    earlier = (row < col).astype(f32).astype(bf16)
    later_mat = (row > col).astype(f32).astype(bf16)
    ones = jnp.ones((S, S), bf16)
    half = jnp.concatenate([earlier, ones], axis=1)
    tri[...] = jnp.concatenate([half, half], axis=0)
    tril[...] = jnp.concatenate([later_mat, later_mat], axis=0)
    ones2[...] = jnp.ones((2 * feats, feats), bf16)
    cur_l[...] = logit_ref[...]

    def tile_copy(v, k, src, dst, send, recv):
        return pltpu.make_async_remote_copy(
            src_ref=src.at[v, tile_peer(k)], dst_ref=dst.at[v, me_t],
            send_sem=send.at[v, k], recv_sem=recv.at[v, k],
            device_id=(tile_peer(k), me_d), device_id_type=pl.DeviceIdType.MESH,
        )

    def exchange(v, moves, beside=None):
        for k in range(owners - 1, 0, -1):
            for move in moves:
                tile_copy(v, k, *move).start()
        for src, dst, _, _ in moves:
            dst[v, me_t] = src[v, me_t]
        if beside is not None:
            beside()
        for k in range(1, owners):
            for move in moves:
                tile_copy(v, k, *move).wait()

    def spread(ref, v, eight):
        for t in range(owners):
            block = eight[:, (t // per) * lanes : (t // per + 1) * lanes]
            turn = (t % per) * cap
            ref[v, t] = pltpu.roll(block, lanes - turn, 1) if turn else block

    def join(ref, v):
        place = iota((8, lanes), 1) // cap
        blocks = []
        for first in range(0, owners, per):
            block = ref[v, first]
            for turn in range(1, per):
                moved = pltpu.roll(ref[v, first + turn], turn * cap, 1)
                block = jnp.where(place == turn, moved, block)
            blocks.append(block)
        return jnp.concatenate(blocks, axis=1)

    def depth_copy(v, k, src, dst, src_at, send, recv):
        return pltpu.make_async_remote_copy(
            src_ref=src.at[v, src_at], dst_ref=dst.at[v, me_d],
            send_sem=send.at[v, k], recv_sem=recv.at[v, k],
            device_id=(me_t, depth_peer(k)), device_id_type=pl.DeviceIdType.MESH,
        )

    def image_copy(v):
        return pltpu.make_async_remote_copy(
            src_ref=img_out.at[v], dst_ref=img_in.at[v],
            send_sem=i_send.at[v], recv_sem=i_recv.at[v],
            device_id=(me_t, partner), device_id_type=pl.DeviceIdType.MESH,
        )

    def slot_rows(v, e):
        g = gath_s[v, e]
        coef_a = jnp.exp(g[2:3])
        coef_c = jnp.exp(g[3:4])
        spread = jnp.exp(0.5 * (g[2:3] + g[3:4]))
        return g[0:1], g[1:2], coef_a, g[4:5] * spread, coef_c, spread, g[5:6]

    def forward(v, e):
        g0, g1, ca, cb, cc, _, opacity = slot_rows(v, e)
        dx = places[0] - g0
        dy = places[1] - g1
        quadric = ca * dx * dx + 2.0 * cb * dx * dy + cc * dy * dy
        fall = jnp.exp(-0.5 * quadric)
        coverage = jnp.minimum(opacity * fall, clamp_top)
        log_keep = jnp.log(1.0 - coverage)
        sums = dot(two_parts(log_keep), tri[...])
        decayed = jnp.exp(sums[:, :S])
        weights = (coverage * decayed).astype(bf16)
        fall_s[e] = fall
        dec_s[e] = decayed
        w_s[e] = weights
        keep_s[e] = jnp.exp(sums[:, S:])
        comp_s[e] = dot(weights, gath_f[v, e])

    def combine(v):
        res_s[...] = jnp.zeros((pixels, feats), f32)
        run_s[...] = jnp.ones((pixels, feats), f32)

        def front(e):
            ahead = run_s[...]
            ahead_s[e] = ahead
            res_s[...] = res_s[...] + ahead * comp_s[e]
            run_s[...] = ahead * keep_s[e]

        steps(0, layers, front)
        summed = res_s[...]
        img_ref[v, my_tile] = summed[:share].T.astype(bf16)
        img_out[v] = summed[share:].T.astype(bf16)
        for h in range(tiles):
            target_copy(v, h).wait()
            res_s[h * share : (h + 1) * share] = summed[
                h * share : (h + 1) * share
            ] - tgt[v, h].astype(f32).T
        run_s[...] = jnp.zeros((pixels, feats), f32)

        def rear(i):
            e = layers - 1 - i
            behind = run_s[...]
            keep = keep_s[e]
            gk_s[e] = ahead_s[e] * behind * keep
            terms = dot(two_parts(res_s[...] * comp_s[e]), ones2[...])
            run_s[...] = terms + keep * behind

        steps(0, layers - 1, rear)
        gk_s[0] = ahead_s[0] * run_s[...] * keep_s[0]

    def backward(v, e, out_f, out_s):
        g0, g1, ca, cb, cc, spread, opacity = slot_rows(v, e)
        grad_comp = (ahead_s[e] * res_s[...]).astype(bf16)
        out_f[v, e] = dot(w_s[e], grad_comp, 0, 0).astype(bf16)
        grad_weight = dot(grad_comp, gath_f[v, e], 1, 1)
        decayed = dec_s[e]
        fall = fall_s[e]
        product = opacity * fall
        coverage = jnp.minimum(product, clamp_top)
        grad_decayed = grad_weight * decayed
        later = dot(two_parts(grad_decayed * coverage), tril[...])
        grad_log = later + gk_s[e]
        grad_coverage = grad_decayed - grad_log / (1.0 - coverage)
        moment = fall * jnp.where(product < clamp_top, grad_coverage, 0.0)
        dx = places[0] - g0
        dy = places[1] - g1
        moment_x = moment * dx
        moment_y = moment * dy

        def total(value):
            return jnp.sum(value, axis=0, keepdims=True)

        m0 = total(moment)
        mx = opacity * total(moment_x)
        my = opacity * total(moment_y)
        first = -0.5 * opacity * total(moment_x * dx)
        cross = -1.0 * opacity * total(moment_x * dy)
        second = -0.5 * opacity * total(moment_y * dy)
        out_s[v, e] = put_rows(
            [
                ca * mx + cb * my,
                cb * mx + cc * my,
                ca * first + 0.5 * cb * cross,
                cc * second + 0.5 * cb * cross,
                spread * cross,
                opacity * (1.0 - opacity) * m0,
            ],
            (8, S),
        )

    def move_rows(eight, onehot, side):
        high, mid, low = three_parts(eight)
        rows = jnp.concatenate([high, mid, low, jnp.zeros_like(low)], axis=0)
        moved = dot(rows.astype(bf16), onehot, 1, side)
        return moved[0:8] + moved[8:16] + moved[16:24]

    def pack(ref, v, value):
        ref[v] = value.reshape(owners, cap, feats).astype(wire)

    def unpack(ref, v):
        return ref[v].astype(f32).reshape(owned, feats).astype(bf16)

    def indices(v):
        dest = dest_ref[v]
        low_edge = iota((owners, owned), 0) * owned
        hit = (dest >= low_edge) & (dest < low_edge + owned)
        matches = hit.astype(f32)
        upper = (iota((owned, owned), 0) < iota((owned, owned), 1)).astype(f32).astype(bf16)
        rank = dot(matches.astype(bf16), upper)
        count = iota((owners, owned), 0).astype(f32) * cap + rank + 1.0
        position = jnp.sum(matches * count, axis=0, keepdims=True) - 1.0
        ids[v] = jnp.sum(
            matches * (dest - low_edge + 1).astype(f32), axis=0, keepdims=True
        )
        perm[v] = (iota((owned, owned), 0).astype(f32) == position).astype(f32).astype(bf16)

    def dispatch(v):
        opacity = 1.0 / (1.0 + jnp.exp(-cur_l[...]))
        rows8 = iota((8, owned), 0)
        eight = jnp.where(rows8 == 5, opacity, jnp.where(rows8 == 6, ids[v], geom8[v]))
        pack(pay, v, dot(perm[v], cur_f[...]))
        spread(pay_s, v, move_rows(eight, perm[v], 1))

    def later_indices():
        for v in range(1, views):
            indices(v)

    indices(0)
    feature_copy.wait()
    for v in range(views):
        dispatch(v)
        if v == 0:
            pl.semaphore_wait(barrier, owners + layers - 2)
        exchange(
            v,
            [(pay_s, got_s, as_send, as_recv), (pay, got, a_send, a_recv)],
            later_indices if v == 0 else None,
        )
        arrived = join(got_s, v)
        slots = (iota((owned, owned), 0).astype(f32) + 1.0 == arrived[6:7, :]).astype(f32).astype(bf16)
        to_slot[v] = slots
        slot_f = dot(slots, unpack(got, v)).astype(bf16)
        shapes = move_rows(arrived, slots, 1)
        for t in range(tiles):
            mine_f[v, t] = slot_f[t * S : (t + 1) * S]
            mine_s[v, t] = shapes[:, t * S : (t + 1) * S]

        def gather(k):
            there = depth_peer(k) // group
            return (
                depth_copy(v, k, mine_f, gath_f, there, gf_send, gf_recv),
                depth_copy(v, k, mine_s, gath_s, there, gs_send, gs_recv),
            )

        for k in range(layers - 1, 0, -1):
            for copy in gather(k):
                copy.start()
        gath_f[v, me_d] = mine_f[v, my_tile]
        gath_s[v, me_d] = mine_s[v, my_tile]
        forward(v, me_d)

        def fwd_step(i):
            k = layers - i
            for copy in gather(k):
                copy.wait()
            forward(v, depth_peer(k))

        steps(1, layers, fwd_step)
        combine(v)

        def give(k):
            e = depth_peer(k)
            return (
                depth_copy(v, k, part_f, in_f, e, pf_send, pf_recv),
                depth_copy(v, k, part_s, in_s, e, ps_send, ps_recv),
            )

        def bwd_step(i):
            k = layers - i
            backward(v, depth_peer(k), part_f, part_s)
            for copy in give(k):
                copy.start()

        steps(1, layers, bwd_step)
        image_copy(v).start()
        backward(v, me_d, in_f, in_s)
        for k in range(1, layers):
            for copy in give(k):
                copy.wait()
        sums_f = []
        sums_s = []
        for t in range(tiles):
            sums_f.append(sum(in_f[v, z].astype(f32) for z in range(t * group, (t + 1) * group)))
            sums_s.append(sum(in_s[v, z] for z in range(t * group, (t + 1) * group)))
        sum_f = jnp.concatenate(sums_f, axis=0)
        sum_s = jnp.concatenate(sums_s, axis=1)
        pack(back, v, dot(to_slot[v], sum_f.astype(bf16), 0, 0))
        spread(back_s, v, move_rows(sum_s, to_slot[v], 0))
        exchange(v, [(back, ret, b_send, b_recv), (back_s, ret_s, bs_send, bs_recv)])
        grad_feat = dot(perm[v], unpack(ret, v), 0, 0)
        grad_eight = move_rows(join(ret_s, v), perm[v], 0)
        sg_ref[v] = grad_eight
        cur_f[...] = (cur_f[...].astype(f32) - feature_rate * grad_feat).astype(bf16)
        cur_l[...] = cur_l[...] - opacity_rate * grad_eight[5:6]

    for v in range(views):
        image_copy(v).wait()
        img_ref[v, 1 - my_tile] = img_in[v]
    newf_ref[...] = cur_f[...]
    newl_ref[...] = cur_l[...]


def body(features, logits, geometry, dest_slot, target):
    owners = lax.axis_size("tile")
    layers = lax.axis_size("depth")
    depth_here = lax.axis_index("depth")
    views, tiles, feats, pixels = target.shape
    owned = features.shape[1]
    cap = owned // owners
    share = pixels // layers
    wire = bf16 if cap % 16 == 0 else f32
    if tiles != 2 or layers % tiles or 128 % cap or layers & (layers - 1) or owners & (owners - 1):
        raise ValueError("unsupported split")
    if share % 128:
        group = layers // tiles
        tile_here = depth_here // group
        partner = lax.rem(depth_here + group, layers)
        target = jnp.concatenate(
            [
                lax.dynamic_slice(
                    target, (0, tile_here, 0, place * share), (views, 1, feats, share)
                )
                for place in (depth_here, partner)
            ],
            axis=1,
        )
    hbm = pl.BlockSpec(memory_space=pl.ANY)
    vm = pl.BlockSpec(memory_space=pltpu.VMEM)
    grid = (layers, tiles * share, S)
    dma = pltpu.SemaphoreType.DMA
    images, new_f, new_l, grads = pl.pallas_call(
        functools.partial(splat_kernel, owners, layers, views, tiles, share),
        out_shape=(
            jax.ShapeDtypeStruct((views, tiles, feats, share), bf16),
            jax.ShapeDtypeStruct((owned, feats), bf16),
            jax.ShapeDtypeStruct((1, owned), f32),
            jax.ShapeDtypeStruct((views, 8, owned), f32),
        ),
        in_specs=[hbm, vm, vm, vm, hbm],
        out_specs=(vm,) * 4,
        scratch_shapes=[
            pltpu.VMEM((views, owners, cap, feats), wire),
            pltpu.VMEM((views, owners, cap, feats), wire),
            pltpu.VMEM((views, owners, cap, feats), wire),
            pltpu.VMEM((views, owners, cap, feats), wire),
            pltpu.VMEM((views, owners, 8, 128), f32),
            pltpu.VMEM((views, owners, 8, 128), f32),
            pltpu.VMEM((views, owners, 8, 128), f32),
            pltpu.VMEM((views, owners, 8, 128), f32),
            pltpu.VMEM((views, 8, owned), f32),
            pltpu.VMEM((views, tiles, feats, share), bf16),
            pltpu.VMEM((views, tiles, S, feats), bf16),
            pltpu.VMEM((views, tiles, 8, S), f32),
            pltpu.VMEM((views, layers, S, feats), bf16),
            pltpu.VMEM((views, layers, 8, S), f32),
            pltpu.VMEM((views, layers, S, feats), bf16),
            pltpu.VMEM((views, layers, 8, S), f32),
            pltpu.VMEM((views, layers, S, feats), bf16),
            pltpu.VMEM((views, layers, 8, S), f32),
            pltpu.VMEM((views, feats, share), bf16),
            pltpu.VMEM((views, feats, share), bf16),
            pltpu.VMEM((views, owned, owned), bf16),
            pltpu.VMEM((views, 1, owned), f32),
            pltpu.VMEM((views, owned, owned), bf16),
            pltpu.VMEM((2, tiles * share, S), f32),
            pltpu.VMEM((2 * S, 2 * S), bf16),
            pltpu.VMEM((2 * S, S), bf16),
            pltpu.VMEM((2 * feats, feats), bf16),
            pltpu.VMEM(grid, f32),
            pltpu.VMEM(grid, f32),
            pltpu.VMEM(grid, bf16),
            pltpu.VMEM(grid, f32),
            pltpu.VMEM(grid, f32),
            pltpu.VMEM(grid, f32),
            pltpu.VMEM(grid, f32),
            pltpu.VMEM((tiles * share, feats), f32),
            pltpu.VMEM((tiles * share, feats), f32),
            pltpu.VMEM((owned, feats), bf16),
            pltpu.VMEM((1, owned), f32),
            dma((views, owners)), dma((views, owners)),
            dma((views, layers)), dma((views, layers)),
            dma((views, layers)), dma((views, layers)),
            dma((views, layers)), dma((views, layers)),
            dma((views, layers)), dma((views, layers)),
            dma((views, owners)), dma((views, owners)),
            dma((views,)), dma((views,)),
            dma((views, owners)), dma((views, owners)),
            dma((views, owners)), dma((views, owners)),
            dma((1 + views * tiles,)),
        ],
        compiler_params=pltpu.CompilerParams(
            collective_id=0, has_side_effects=True, vmem_limit_bytes=56 * 1024 * 1024
        ),
        name="splat_views",
    )(features[0], logits, geometry.transpose(0, 2, 1, 3), dest_slot, target)
    images, new_f, new_l, grads = pl.pallas_call(
        finish_kernel,
        out_shape=(
            jax.ShapeDtypeStruct(images.shape, bf16),
            jax.ShapeDtypeStruct((1, owned, feats), bf16),
            jax.ShapeDtypeStruct((1, owned), f32),
            jax.ShapeDtypeStruct((views, 5, 1, owned), f32),
        ),
        in_specs=[vm] * 4,
        out_specs=(vm,) * 4,
        name="write_outputs",
    )(images, new_f, new_l, grads)
    return images, new_f, new_l, grads.transpose(0, 2, 1, 3)


def solution(mesh):
    placed = (
        P("depth", "tile", None),
        P("depth", "tile"),
        P(None, "depth", None, "tile"),
        P(None, "depth", "tile"),
        P(None, "tile", None, None),
    )
    return jax.shard_map(
        body,
        mesh=mesh,
        in_specs=placed,
        out_specs=(
            P(None, "tile", None, "depth"),
            P("depth", "tile", None),
            P("depth", "tile"),
            P(None, "depth", None, "tile"),
        ),
        check_vma=False,
    )
```
